256 devices in a mesh: epoch: 16 (over z, y_lo), col: 16 (over x, y_hi, core).
Axes of the slice: x: 4, y: 4 (y_hi: 2, y_lo: 2; y = y_hi * 2 + y_lo), z: 8, core: 2. Of those that a mesh axis runs over, the one named last changes fastest.
Arguments:
- partials: bfloat16 [4096, 8192], P('epoch', 'col'), may hold values from -6 to 6
- gaps: int32 [4096], P('epoch'), may hold values 0 or 1
- arc_start: int32 [1], replicated, may hold values from 1024 to 3071
- taps: bfloat16 [241], replicated, may hold values from -0.375 to 0.375
Outputs:
- normal_matrix: float32 [8192, 8192], P('col', 'epoch')
The draws below stay inside these ranges and needn't reach their ends.
All inputs are finite; a program needn't handle non-finite values. No bound on the sum of `gaps` on one device may be relied on, other than what follows from the above.
Results may differ from the reference program's by a relative error of at most 0.0026.
Values may be sent and summed in bfloat16 or wider, within the bound.
No kernel may reach another device: no remote copies, remote signals or barrier semaphores. Data moves between devices by JAX's collectives and lax.ppermute only.
A program may use at most 64 MiB of HBM per device.

```python
import jax
import jax.numpy as jnp
from jax import lax

P_SIZE = 8192
TAPS = 241
E_DEV = 256
EPOCHS = 4096


def plant(drawn, key, least, largest):
    extent = drawn.shape
    place = [jax.random.randint(jax.random.fold_in(key, axis), (), 0, extent[axis]) for axis in range(len(extent))]
    drawn = drawn.at[tuple(place)].set(least)
    longest = extent.index(max(extent))
    place[longest] = (place[longest] + 1) % extent[longest]
    return drawn.at[tuple(place)].set(largest)


def strengthened(values, key, source, target, parts, factor):
    owner, partner = [(jnp.arange(values.shape[dim]) // (values.shape[dim] // parts)).reshape([-1 if axis == dim else 1 for axis in range(values.ndim)]) for dim in (source, target)]
    chosen = jax.random.permutation(key, parts)[partner]
    strong = (owner == chosen) | (owner == (partner + parts // 2) % parts)
    return jnp.where(strong, factor * values, values)


def steps_of(rng, dims, split, smallest, high):
    gain, own = 1.0, jax.random.fold_in(rng, 6)
    for position, blocks in split:
        steps = jnp.exp(jax.random.uniform(jax.random.fold_in(own, position), (blocks,), jnp.float32, smallest / len(split), high / len(split)))
        gain = gain * jnp.repeat(steps, dims[position] // blocks).reshape([-1 if axis == position else 1 for axis in range(len(dims))])
    return gain


def gaussian(own_key, shape, scale, limit, shards=(), kind=jnp.bfloat16):
    factor_of = steps_of(own_key, shape, shards, -0.22, 0.18) if shards else 1.0
    result = jax.random.normal(own_key, shape, jnp.float32) * scale * factor_of
    return jnp.minimum(jnp.maximum(result, -limit), limit).astype(kind)


def bell_draw_with(own_key, shape, spread, limit, cuts, heavy, kind=jnp.bfloat16):
    drawn = spread * jax.random.normal(own_key, shape, jnp.float32)
    if cuts:
        drawn = drawn * steps_of(own_key, shape, cuts, -0.22, 0.18)
    return jnp.clip(strengthened(drawn, jax.random.fold_in(own_key, 3), *heavy), -limit, limit).astype(kind)


def setup_inputs(seed: int = 0) -> dict:
    keys = jax.random.split(jax.random.key(seed), 5)
    partials = bell_draw_with(keys[0], (EPOCHS, P_SIZE), 1.0, 6.0, ((0, 16), (1, 16)), (0, 1, 16, 2.0))
    gaps = plant((jax.random.randint(keys[1], (EPOCHS,), 0, 8) < 7).astype(jnp.int32), jax.random.fold_in(keys[1], 1), 0, 1)
    arc_start = jax.random.randint(keys[2], (1,), EPOCHS // 4, 3 * EPOCHS // 4).astype(jnp.int32)
    taps = gaussian(keys[3], (TAPS,), TAPS ** -0.5, 0.375)
    return dict(partials=partials, gaps=gaps, arc_start=arc_start, taps=taps)


def filter_table(first, rows, halo, taps, boundary):
    width = rows + halo
    padded_taps = jnp.concatenate([taps[::-1], jnp.zeros((rows,), taps.dtype)], axis=0)
    values = jnp.tile(padded_taps, rows)[: rows * width].reshape(rows, width)
    later = jnp.arange(rows, dtype=jnp.int32)
    source = jnp.arange(width, dtype=jnp.int32)
    lag = later[:, None] + halo - source[None, :]
    arc_later = (first + later) >= boundary
    arc_source = (first - halo + source) >= boundary
    keep = (lag >= 0) & (lag <= halo) & (arc_later[:, None] == arc_source[None, :])
    return jnp.where(keep, values, jnp.zeros_like(values))


def reference(partials, gaps, arc_start, taps):
    halo = TAPS - 1
    masked = partials * gaps[:, None].astype(jnp.bfloat16)
    padded = jnp.concatenate([jnp.zeros((halo, P_SIZE), jnp.bfloat16), masked], axis=0)

    def one_block(block):
        first = (block * E_DEV).astype(jnp.int32)
        stacked = lax.dynamic_slice_in_dim(padded, first, E_DEV + halo, 0)
        table = filter_table(first, E_DEV, halo, taps, arc_start[0])
        return jnp.dot(table, stacked, preferred_element_type=jnp.float32).astype(jnp.bfloat16)

    white = lax.map(one_block, jnp.arange(EPOCHS // E_DEV, dtype=jnp.int32)).reshape(EPOCHS, P_SIZE)
    gram = jnp.dot(white.T, white, preferred_element_type=jnp.float32)
    return gram * (EPOCHS ** -0.5)
```

```python
import functools

import jax
import jax.numpy as jnp
from jax import lax
from jax.experimental import pallas as pl
from jax.experimental.pallas import tpu as pltpu
from jax.sharding import Mesh, PartitionSpec as P

NZ, NYL, NX, NYH, NC = 8, 2, 4, 2, 2
EPOCH = ("z", "yl")
COL = ("x", "yh", "c")
BF16, F32 = jnp.bfloat16, jnp.float32


def ring(n, step):
    return [(i, (i + step) % n) for i in range(n)]


def around(block, axis, n, step):
    return lax.ppermute(block, axis, ring(n, step))


def transposing_route():
    route = []
    for z_from in range(NZ):
        for x_from in range(NX):
            for yh_from in range(NYH):
                z = 2 * x_from + yh_from
                g = (z_from - z if z % 2 == 0 else z - z_from) % NZ
                x, yh = g // 2, g % 2
                route.append(((z_from * NX + x_from) * NYH + yh_from, (z * NX + x) * NYH + yh))
    return route


def filter_table(first, rows, halo, taps, boundary):
    width = rows + halo
    padded_taps = jnp.concatenate([taps[::-1], jnp.zeros((rows,), taps.dtype)], axis=0)
    values = jnp.tile(padded_taps, rows)[: rows * width].reshape(rows, width)
    later = jnp.arange(rows, dtype=jnp.int32)
    source = jnp.arange(width, dtype=jnp.int32)
    lag = later[:, None] + halo - source[None, :]
    arc_later = first + later >= boundary
    arc_source = first - halo + source >= boundary
    keep = (lag >= 0) & (lag <= halo) & (arc_later[:, None] == arc_source[None, :])
    return jnp.where(keep, values, jnp.zeros_like(values))


def gram_kernel(scale, index_ref, *refs):
    left = refs[0:8]
    right = refs[8:16]
    keep_ref, send_ref, left_all, right_all, sems = refs[16:]
    rows = right[0].shape[0] // 2
    copies = []
    for d in range(8):
        copies.append(pltpu.make_async_copy(left[d], left_all.at[:, pl.ds(d * rows, rows)], sems.at[d]))
    for q in range(2):
        for s in range(4):
            for h in range(2):
                n = (q * 4 + s) * 2 + h
                start = pl.multiple_of(index_ref[s * 2 + h] * rows, rows)
                target = right_all.at[index_ref[8 + q], pl.ds(start, rows), :]
                copies.append(pltpu.make_async_copy(right[q * 4 + s].at[pl.ds(h * rows, rows), :], target, sems.at[8 + n]))
    for copy in copies:
        copy.start()
    for copy in copies:
        copy.wait()
    send_ref[...] = (jnp.dot(left_all[...], right_all[1], preferred_element_type=F32) * scale).astype(BF16)
    keep_ref[...] = jnp.dot(left_all[...], right_all[0], preferred_element_type=F32) * scale


def gram(index, left, right, scale):
    cols, rows = left[0].shape
    return pl.pallas_call(
        functools.partial(gram_kernel, scale),
        out_shape=[jax.ShapeDtypeStruct((cols, cols), F32), jax.ShapeDtypeStruct((cols, cols), BF16)],
        in_specs=[pl.BlockSpec(memory_space=pltpu.SMEM)] + [pl.BlockSpec(memory_space=pl.ANY)] * 16,
        out_specs=[pl.BlockSpec(memory_space=pltpu.VMEM)] * 2,
        scratch_shapes=[
            pltpu.VMEM((cols, 8 * rows), BF16),
            pltpu.VMEM((2, 8 * rows, cols), BF16),
            pltpu.SemaphoreType.DMA((24,)),
        ],
        compiler_params=pltpu.CompilerParams(vmem_limit_bytes=32 * 1024 * 1024),
        name="gram",
    )(index, *left, *right)


def on_device(partials, gaps, arc_start, taps):
    rows = partials.shape[0]
    halo = taps.shape[0] - 1
    masked = partials * gaps[:, None].astype(BF16)
    epochs = range(NZ * NYL)
    earlier = lax.ppermute(masked[rows - halo :], EPOCH, [(e, e + 1) for e in epochs if e + 1 in epochs])
    z, yl = lax.axis_index("z"), lax.axis_index("yl")
    x, yh, core = lax.axis_index("x"), lax.axis_index("yh"), lax.axis_index("c")
    first = (z * NYL + yl) * rows
    table = filter_table(first, rows, halo, taps, arc_start[0])
    stacked = jnp.concatenate([earlier, masked], axis=0)
    white = jnp.dot(table, stacked, preferred_element_type=F32).astype(BF16)
    white_t = lax.dot_general(stacked, table, (((0,), (1,)), ((), ())), preferred_element_type=F32).astype(BF16)

    here = lax.ppermute(white, ("z", "x", "yh"), transposing_route())
    pair = jnp.concatenate([here, around(here, "yh", NYH, 1)], axis=0)
    x_up = around(pair, "x", NX, 1)
    x_down = around(pair, "x", NX, -1)
    x_far = jnp.concatenate([around(x_up[:rows], "x", NX, 1), around(x_down[rows:], "x", NX, -1)], axis=0)
    own = [pair, x_up, x_down, x_far]
    other = [around(piece, "c", NC, 1) for piece in own]

    left = [None] * NZ
    left[0] = up = down = white_t
    for step in range(1, 4):
        up = around(up, "z", NZ, 1)
        down = around(down, "z", NZ, -1)
        left[NZ - step], left[step] = up, down
    half = white_t.shape[0] // 2
    left[4] = jnp.concatenate([around(up[:half], "z", NZ, 1), around(down[half:], "z", NZ, -1)], axis=0)

    sign = jnp.where(z % 2 == 0, 1, -1)
    places = [
        (sign * (2 * ((x + dx) % NX) + (yh + dy) % NYH)) % NZ
        for dx in (0, -1, 1, 2)
        for dy in (0, 1)
    ]
    swapped = jnp.where(core == yl, 0, 1)
    index = jnp.stack(places + [swapped, 1 - swapped]).astype(jnp.int32)
    scale = (rows * NZ * NYL) ** (-0.5)
    keep, send = gram(index, left, own + other, scale)
    return keep + around(send, "yl", NYL, 1).astype(F32)


def solution(mesh):
    fine = Mesh(mesh.devices.reshape(NZ, NYL, NX, NYH, NC), EPOCH + COL)
    in_specs = (P(EPOCH, COL), P(EPOCH), P(), P())
    return jax.shard_map(on_device, mesh=fine, in_specs=in_specs, out_specs=P(COL, EPOCH), check_vma=False)
```

```python
import functools

import jax
import jax.numpy as jnp
from jax import lax
from jax.experimental import pallas as pl
from jax.experimental.pallas import tpu as pltpu
from jax.sharding import Mesh, PartitionSpec as P

NZ, NYL, NX, NYH, NC = 8, 2, 4, 2, 2
EPOCH = ("z", "yl")
COL = ("x", "yh", "c")
NE = NZ * NYL
BF16, F32 = jnp.bfloat16, jnp.float32
DX = (0, -1, 1, 2)
LEFT_Z = (0, -1, 1, -2, 2, -3, 3)


def around(block, axis, n, step):
    return lax.ppermute(block, axis, [(i, (i + step) % n) for i in range(n)])


def line_of(z_from, z, half):
    return (z_from + z + half * (NZ // 2)) % NZ


def in_plane(block, half):
    axes = ("z", "yl", "x", "yh", "c")
    sizes = (NZ, NYL, NX, NYH, NC)

    def flat(place):
        index = 0
        for size, at in zip(sizes, place):
            index = index * size + at
        return index

    route = []
    for z in range(NZ):
        for yl in range(NYL):
            for x in range(NX):
                for yh in range(NYH):
                    for c in range(NC):
                        line = line_of(z, NYH * x + yh, half)
                        route.append((flat((z, yl, x, yh, c)), flat((z, c, line // NYH, line % NYH, yl))))
    return lax.ppermute(block, axes, route)


def along_z(block, half):
    route = []
    for z_from in range(NZ):
        for z in range(NZ):
            line = line_of(z_from, z, half)
            route.append(((z_from * NX + line // NYH) * NYH + line % NYH, (z * NX + line // NYH) * NYH + line % NYH))
    return lax.ppermute(block, ("z", "x", "yh"), route)


def filter_tables(rows, taps, boundary):
    width = 2 * rows
    padded_taps = jnp.concatenate([jnp.zeros((rows + 1 - taps.shape[0],), taps.dtype), taps[::-1], jnp.zeros((rows,), taps.dtype)])
    values = jnp.tile(padded_taps, rows)[: rows * width].reshape(rows, width)
    later = jnp.arange(rows, dtype=jnp.int32)[:, None]
    source = jnp.arange(width, dtype=jnp.int32)[None, :]
    lag = later + rows - source
    base = jnp.where((lag >= 0) & (lag <= rows), values, jnp.zeros_like(values))
    tables = [base]
    for block in (boundary // rows, boundary // rows + 1):
        split = (block * rows + later >= boundary) & ((block - 1) * rows + source < boundary)
        tables.append(jnp.where(split, jnp.zeros_like(base), base))
    return jnp.stack(tables)


def prepare_kernel(partials_ref, gaps_ref, first_ref, second_ref, turned_ref):
    rows, cols = partials_ref.shape
    kept = jnp.broadcast_to(gaps_ref[...].astype(F32), (128, rows))
    kept_t = kept.T.astype(BF16)
    for i in range(cols // 128):
        part = partials_ref[:, i * 128 : (i + 1) * 128] * kept_t
        turned_ref[i * 128 : (i + 1) * 128, :] = part.T
        half = (first_ref, second_ref)[i // (cols // 256)]
        at = i % (cols // 256) * 128
        half[:, at : at + 128] = part


def prepare(partials, gaps):
    rows, cols = partials.shape
    return pl.pallas_call(
        prepare_kernel,
        out_shape=[jax.ShapeDtypeStruct((rows, cols // 2), BF16)] * 2 + [jax.ShapeDtypeStruct((cols, rows), BF16)],
        name="prepare",
    )(partials, gaps[None, :])


def gram_kernel(scale, meta_ref, tables_ref, tables_t_ref, *refs):
    left_near, left_far, right = refs[0:7], refs[7:9], refs[9:17]
    out_ref, raw_left, raw_right, white_left, white_right = refs[17:]
    rows = raw_left.shape[2]
    cols = raw_left.shape[1]
    z, yl, x, yh, core, cut = [meta_ref[i] for i in range(6)]
    raw_left[0] = jnp.zeros(raw_left.shape[1:], BF16)
    for h in range(2):
        raw_right[h, 0] = jnp.zeros(raw_right.shape[2:], BF16)
    for dz, piece in zip(LEFT_Z, left_near):
        for b in range(2):
            raw_left[2 * ((z + dz) & 7) + (yl ^ b) + 1] = piece[b * cols : (b + 1) * cols]
    for b in range(2):
        raw_left[2 * ((z + 4) & 7) + (yl ^ b) + 1] = left_far[b][...]
    for q in range(2):
        for s in range(4):
            for b in range(4):
                line = NYH * ((x + DX[s]) & 3) + (yh ^ (b // 2))
                e = 2 * ((line - z + (b % 2) * (NZ // 2)) & 7) + (core ^ q)
                raw_right[b % 2, e + 1] = right[q * 4 + s][b * rows : (b + 1) * rows]

    @pl.loop(0, NE)
    def _(e):
        which = jnp.where(e == cut, 1, jnp.where(e == cut + 1, 2, 0))
        table_t = tables_t_ref[which]
        table = tables_ref[which]
        at = pl.multiple_of(e * rows, rows)
        left = jnp.dot(raw_left[e], table_t[:rows], preferred_element_type=F32)
        left += jnp.dot(raw_left[e + 1], table_t[rows:], preferred_element_type=F32)
        white_left[:, pl.ds(at, rows)] = left.astype(BF16)
        for h in range(2):
            right_h = jnp.dot(table[:, :rows], raw_right[h, e], preferred_element_type=F32)
            right_h += jnp.dot(table[:, rows:], raw_right[h, e + 1], preferred_element_type=F32)
            white_right[pl.ds(at, rows), pl.ds(h * rows, rows)] = right_h.astype(BF16)

    out_ref[...] = jnp.dot(white_left[...], white_right[...], preferred_element_type=F32) * scale


def gram(meta, tables, tables_t, left_near, left_far, right, rows, cols, scale):
    vmem = pl.BlockSpec(memory_space=pltpu.VMEM)
    return pl.pallas_call(
        functools.partial(gram_kernel, scale),
        out_shape=jax.ShapeDtypeStruct((cols, cols), F32),
        in_specs=[pl.BlockSpec(memory_space=pltpu.SMEM)] + [vmem] * 19,
        out_specs=vmem,
        scratch_shapes=[
            pltpu.VMEM((NE + 1, cols, rows), BF16),
            pltpu.VMEM((2, NE + 1, rows, rows), BF16),
            pltpu.VMEM((cols, NE * rows), BF16),
            pltpu.VMEM((NE * rows, cols), BF16),
        ],
        compiler_params=pltpu.CompilerParams(vmem_limit_bytes=24 * 1024 * 1024),
        name="gram",
    )(meta, tables, tables_t, *left_near, *left_far, *right)


def on_device(partials, gaps, arc_start, taps):
    rows, cols = partials.shape
    z, yl = lax.axis_index("z"), lax.axis_index("yl")
    x, yh, core = lax.axis_index("x"), lax.axis_index("yh"), lax.axis_index("c")
    first, second, masked_t = prepare(partials, gaps)

    both = jnp.concatenate([masked_t, around(masked_t, "yl", NYL, 1)], axis=0)
    left_near = [both]
    up = down = both
    for step in range(1, 4):
        up = around(up, "z", NZ, 1)
        down = around(down, "z", NZ, -1)
        left_near += [up, down]
    left_far = [around(up[:cols], "z", NZ, 1), around(down[cols:], "z", NZ, -1)]

    halves = [along_z(in_plane(piece, h), h) for h, piece in enumerate((first, second))]
    here = jnp.concatenate(halves, axis=0)
    pair = jnp.concatenate([here, around(here, "yh", NYH, 1)], axis=0)
    x_up = around(pair, "x", NX, 1)
    x_down = around(pair, "x", NX, -1)
    x_far = jnp.concatenate([around(x_up[: 2 * rows], "x", NX, 1), around(x_down[2 * rows :], "x", NX, -1)], axis=0)
    own = [pair, x_up, x_down, x_far]
    other = [around(piece, "c", NC, 1) for piece in own]

    boundary = arc_start[0]
    tables = filter_tables(rows, taps, boundary)
    tables_t = tables.transpose(0, 2, 1)

    meta = jnp.stack([z, yl, x, yh, core, boundary // rows]).astype(jnp.int32)
    scale = (rows * NE) ** (-0.5)
    return gram(meta, tables, tables_t, left_near, left_far, own + other, rows, cols, scale)


def solution(mesh):
    fine = Mesh(mesh.devices.reshape(NZ, NYL, NX, NYH, NC), EPOCH + COL)
    in_specs = (P(EPOCH, COL), P(EPOCH), P(), P())
    return jax.shard_map(on_device, mesh=fine, in_specs=in_specs, out_specs=P(COL, EPOCH), check_vma=False)
```

```python
import functools

import jax
import jax.numpy as jnp
from jax import lax
from jax.experimental import pallas as pl
from jax.experimental.pallas import tpu as pltpu
from jax.sharding import Mesh, PartitionSpec as P

NZ, NYL, NX, NYH, NC = 8, 2, 4, 2, 2
EPOCH = ("z", "yl")
COL = ("x", "yh", "c")
NE = NZ * NYL
BF16, F32 = jnp.bfloat16, jnp.float32
DX = (0, -1, 1, 2)
LEFT_Z = (0, -1, 1, -2, 2, -3, 3)


def around(block, axis, n, step):
    return lax.ppermute(block, axis, [(i, (i + step) % n) for i in range(n)])


def line_of(z_from, z, half):
    return (z_from + z + half * (NZ // 2)) % NZ


def in_plane(block, half):
    axes = ("z", "yl", "x", "yh", "c")
    sizes = (NZ, NYL, NX, NYH, NC)

    def flat(place):
        index = 0
        for size, at in zip(sizes, place):
            index = index * size + at
        return index

    route = []
    for z in range(NZ):
        for yl in range(NYL):
            for x in range(NX):
                for yh in range(NYH):
                    for c in range(NC):
                        line = line_of(z, NYH * x + yh, half)
                        route.append((flat((z, yl, x, yh, c)), flat((z, c, line // NYH, line % NYH, yl))))
    return lax.ppermute(block, axes, route)


def along_z(block, half):
    route = []
    for z_from in range(NZ):
        for z in range(NZ):
            line = line_of(z_from, z, half)
            route.append(((z_from * NX + line // NYH) * NYH + line % NYH, (z * NX + line // NYH) * NYH + line % NYH))
    return lax.ppermute(block, ("z", "x", "yh"), route)


def tables_kernel(meta_ref, taps_ref, tables_ref, turned_ref):
    rows, width = tables_ref.shape[1:]
    lags = lax.broadcasted_iota(jnp.int32, (rows, width), 0)
    places = lax.broadcasted_iota(jnp.int32, (rows, width), 1)
    flip = (lags + places == rows).astype(BF16)
    flipped = jnp.dot(jnp.broadcast_to(taps_ref[...], (8, rows)), flip, preferred_element_type=F32)
    base = pltpu.roll(jnp.broadcast_to(flipped[:1], (rows, width)), 0, 1, stride=1, stride_axis=0)
    boundary = meta_ref[5]
    cut = meta_ref[6]
    for i in range(3):
        table = base
        if i:
            first = (cut + i - 1) * rows
            split = (first + lags >= boundary) & (first - rows + places < boundary)
            table = jnp.where(split, 0.0, base)
        tables_ref[i] = table.astype(BF16)
        turned_ref[i] = table.T.astype(BF16)


def make_tables(meta, taps, rows):
    vmem = pl.BlockSpec(memory_space=pltpu.VMEM)
    padded = jnp.pad(taps, (0, rows - taps.shape[0]))[None, :]
    return pl.pallas_call(
        tables_kernel,
        out_shape=[jax.ShapeDtypeStruct((3, rows, 2 * rows), BF16), jax.ShapeDtypeStruct((3, 2 * rows, rows), BF16)],
        in_specs=[pl.BlockSpec(memory_space=pltpu.SMEM), vmem],
        out_specs=[vmem, vmem],
        compiler_params=pltpu.CompilerParams(vmem_limit_bytes=8 * 1024 * 1024),
        name="tables",
    )(meta, padded)


def prepare_kernel(partials_ref, gaps_ref, first_ref, second_ref, turned_ref):
    rows, cols = partials_ref.shape
    kept = jnp.broadcast_to(gaps_ref[...].astype(F32), (128, rows))
    kept_t = kept.T.astype(BF16)
    for i in range(cols // 128):
        part = partials_ref[:, i * 128 : (i + 1) * 128] * kept_t
        turned_ref[i * 128 : (i + 1) * 128, :] = part.T
        half = (first_ref, second_ref)[i // (cols // 256)]
        at = i % (cols // 256) * 128
        half[:, at : at + 128] = part


def prepare(partials, gaps):
    rows, cols = partials.shape
    return pl.pallas_call(
        prepare_kernel,
        out_shape=[jax.ShapeDtypeStruct((rows, cols // 2), BF16)] * 2 + [jax.ShapeDtypeStruct((cols, rows), BF16)],
        compiler_params=pltpu.CompilerParams(vmem_limit_bytes=4 * 1024 * 1024),
        name="prepare",
    )(partials, gaps[None, :])


def table_of(e, meta_ref):
    cut = meta_ref[6]
    return jnp.where(e == cut, 1, jnp.where(e == cut + 1, 2, 0))


def left_kernel(meta_ref, tables_ref, *refs):
    near, far, crossed = refs[0:7], refs[7:9], refs[9:14]
    out_ref, raw = refs[14:]
    cols, rows = raw.shape[1:]
    half = cols // 2
    z, yl = meta_ref[0], meta_ref[1]
    raw[0] = jnp.zeros(raw.shape[1:], BF16)
    for i, dz in enumerate(LEFT_Z):
        at = 2 * ((z + dz) & 7) + 1
        raw[at + yl] = near[i][:cols]
        raw[at + 1 - yl, half:] = near[i][cols:]
        if dz == 0:
            raw[at + 1 - yl, :half] = crossed[0][:half]
        else:
            raw[at + 1 - yl, :half] = crossed[(i + 1) // 2][(i - 1) % 2 * half : ((i - 1) % 2 + 1) * half]
    at = 2 * ((z + 4) & 7) + 1
    split = far[0].shape[0]
    raw[at + yl, :split] = far[0][...]
    raw[at + yl, split:] = far[1][: cols - split]
    raw[at + 1 - yl, half:] = far[1][cols - split :]
    raw[at + 1 - yl, :half] = crossed[4][...]

    @pl.loop(0, NE)
    def _(e):
        table = tables_ref[table_of(e, meta_ref)]
        white = jnp.dot(raw[e], table[:rows], preferred_element_type=F32)
        white += jnp.dot(raw[e + 1], table[rows:], preferred_element_type=F32)
        out_ref[:, pl.ds(pl.multiple_of(e * rows, rows), rows)] = white.astype(BF16)


def right_kernel(meta_ref, tables_ref, *refs):
    pieces = refs[0:8]
    out_ref, raw = refs[8:]
    rows, half = raw.shape[2:]
    z, x, yh, core = [meta_ref[i] for i in (0, 2, 3, 4)]
    for h in range(2):
        raw[h, 0] = jnp.zeros(raw.shape[2:], BF16)
    for q in range(2):
        for s in range(4):
            for b in range(4):
                line = NYH * ((x + DX[s]) & 3) + (yh ^ (b // 2))
                e = 2 * ((line - z + (b % 2) * (NZ // 2)) & 7) + (core ^ q)
                raw[b % 2, e + 1] = pieces[q * 4 + s][b * rows : (b + 1) * rows]

    @pl.loop(0, NE)
    def _(e):
        table = tables_ref[table_of(e, meta_ref)]
        for h in range(2):
            white = jnp.dot(table[:, :rows], raw[h, e], preferred_element_type=F32)
            white += jnp.dot(table[:, rows:], raw[h, e + 1], preferred_element_type=F32)
            out_ref[pl.ds(pl.multiple_of(e * rows, rows), rows), h * half : (h + 1) * half] = white.astype(BF16)


def product_kernel(scale, left_ref, right_ref, out_ref):
    out_ref[...] = jnp.dot(left_ref[...], right_ref[...], preferred_element_type=F32) * scale


def whitened(kernel, name, meta, tables, pieces, shape, raw_shape):
    vmem = pl.BlockSpec(memory_space=pltpu.VMEM)
    return pl.pallas_call(
        kernel,
        out_shape=jax.ShapeDtypeStruct(shape, BF16),
        in_specs=[pl.BlockSpec(memory_space=pltpu.SMEM)] + [vmem] * (1 + len(pieces)),
        out_specs=vmem,
        scratch_shapes=[pltpu.VMEM(raw_shape, BF16)],
        compiler_params=pltpu.CompilerParams(vmem_limit_bytes=16 * 1024 * 1024),
        name=name,
    )(meta, tables, *pieces)


def product(left, right, scale):
    vmem = pl.BlockSpec(memory_space=pltpu.VMEM)
    return pl.pallas_call(
        functools.partial(product_kernel, scale),
        out_shape=jax.ShapeDtypeStruct((left.shape[0], right.shape[1]), F32),
        in_specs=[vmem, vmem],
        out_specs=vmem,
        compiler_params=pltpu.CompilerParams(vmem_limit_bytes=16 * 1024 * 1024),
        name="product",
    )(left, right)


def on_device(partials, gaps, arc_start, taps):
    rows, cols = partials.shape
    half = cols // 2
    places = [lax.axis_index(axis) for axis in EPOCH + COL]
    meta = jnp.stack(places + [arc_start[0], arc_start[0] // rows]).astype(jnp.int32)
    first, second, masked_t = prepare(partials, gaps)

    neighbour = around(masked_t, "yl", NYL, 1)
    up = down = jnp.concatenate([masked_t, neighbour[half:]], axis=0)
    near, crossed = [up], [neighbour]
    for step in range(1, 4):
        if step == 3:
            up, down, crossed[1] = lax.optimization_barrier((up, down, crossed[1]))
        up = around(up, "z", NZ, 1)
        down = around(down, "z", NZ, -1)
        near += [up, down]
        crossed.append(around(jnp.concatenate([up[:half], down[:half]], axis=0), "yl", NYL, 1))
    up, down, crossed[2] = lax.optimization_barrier((up, down, crossed[2]))
    split = (cols + half) // 2
    ends = lax.optimization_barrier((up[:split], down[split:]))
    far = lax.optimization_barrier([around(ends[0], "z", NZ, 1), around(ends[1], "z", NZ, -1)])
    crossed.append(around(far[0][:half], "yl", NYL, 1))

    tables, tables_t = make_tables(meta, taps, rows)
    halves = [along_z(in_plane(piece, h), h) for h, piece in enumerate((first, second))]
    halves, tables, tables_t = lax.optimization_barrier((halves, tables, tables_t))
    here = jnp.concatenate(halves, axis=0)
    pair = jnp.concatenate([here, around(here, "yh", NYH, 1)], axis=0)
    own = [pair] + [around(pair, "x", NX, step) for step in (1, -1, 2)]
    other = [around(piece, "c", NC, 1) for piece in own]

    left = whitened(left_kernel, "left", meta, tables_t, near + far + crossed, (cols, NE * rows), (NE + 1, cols, rows))
    right = whitened(right_kernel, "right", meta, tables, own + other, (NE * rows, cols), (2, NE + 1, rows, half))
    return product(left, right, (rows * NE) ** (-0.5))


def solution(mesh):
    fine = Mesh(mesh.devices.reshape(NZ, NYL, NX, NYH, NC), EPOCH + COL)
    in_specs = (P(EPOCH, COL), P(EPOCH), P(), P())
    return jax.shard_map(on_device, mesh=fine, in_specs=in_specs, out_specs=P(COL, EPOCH), check_vma=False)
```

```python
import functools

import jax
import jax.numpy as jnp
from jax import lax
from jax.experimental import pallas as pl
from jax.experimental.pallas import tpu as pltpu
from jax.sharding import Mesh, PartitionSpec as P

NZ, NYL, NX, NYH, NC = 8, 2, 4, 2, 2
EPOCH = ("z", "yl")
COL = ("x", "yh", "c")
NE = NZ * NYL
BF16, F32 = jnp.bfloat16, jnp.float32
DX = (0, -1, 1, 2)


def around(block, axis, n, step):
    return lax.ppermute(block, axis, [(i, (i + step) % n) for i in range(n)])


def line_of(z_from, z, half):
    return (z_from + z + half * (NZ // 2)) % NZ


def in_plane(block, half):
    axes = ("z", "yl", "x", "yh", "c")
    sizes = (NZ, NYL, NX, NYH, NC)

    def flat(place):
        index = 0
        for size, at in zip(sizes, place):
            index = index * size + at
        return index

    route = []
    for z in range(NZ):
        for yl in range(NYL):
            for x in range(NX):
                for yh in range(NYH):
                    for c in range(NC):
                        line = line_of(z, NYH * x + yh, half)
                        route.append((flat((z, yl, x, yh, c)), flat((z, c, line // NYH, line % NYH, yl))))
    return lax.ppermute(block, axes, route)


def along_z(block, half):
    route = []
    for z_from in range(NZ):
        for z in range(NZ):
            line = line_of(z_from, z, half)
            route.append(((z_from * NX + line // NYH) * NYH + line % NYH, (z * NX + line // NYH) * NYH + line % NYH))
    return lax.ppermute(block, ("z", "x", "yh"), route)


def tables_kernel(meta_ref, taps_ref, tables_ref, turned_ref):
    rows, width = tables_ref.shape[1:]
    lags = lax.broadcasted_iota(jnp.int32, (rows, width), 0)
    places = lax.broadcasted_iota(jnp.int32, (rows, width), 1)
    flip = (lags + places == rows).astype(BF16)
    flipped = jnp.dot(jnp.broadcast_to(taps_ref[...], (8, rows)), flip, preferred_element_type=F32)
    base = pltpu.roll(jnp.broadcast_to(flipped[:1], (rows, width)), 0, 1, stride=1, stride_axis=0)
    boundary = meta_ref[5]
    cut = meta_ref[6]
    for i in range(4):
        table = base
        if i == 3:
            table = jnp.where(places < rows, 0.0, base)
        elif i:
            first = (cut + i - 1) * rows
            split = (first + lags >= boundary) & (first - rows + places < boundary)
            table = jnp.where(split, 0.0, base)
        tables_ref[i] = table.astype(BF16)
        turned_ref[i] = table.T.astype(BF16)


def make_tables(meta, taps, rows):
    vmem = pl.BlockSpec(memory_space=pltpu.VMEM)
    padded = jnp.pad(taps, (0, rows - taps.shape[0]))[None, :]
    return pl.pallas_call(
        tables_kernel,
        out_shape=[jax.ShapeDtypeStruct((4, rows, 2 * rows), BF16), jax.ShapeDtypeStruct((4, 2 * rows, rows), BF16)],
        in_specs=[pl.BlockSpec(memory_space=pltpu.SMEM), vmem],
        out_specs=[vmem, vmem],
        compiler_params=pltpu.CompilerParams(vmem_limit_bytes=8 * 1024 * 1024),
        name="tables",
    )(meta, padded)


def prepare_kernel(partials_ref, gaps_ref, first_ref, second_ref, turned_ref):
    rows, cols = partials_ref.shape
    kept = jnp.broadcast_to(gaps_ref[...].astype(F32), (128, rows))
    kept_t = kept.T.astype(BF16)
    for i in range(cols // 128):
        part = partials_ref[:, i * 128 : (i + 1) * 128] * kept_t
        turned_ref[i * 128 : (i + 1) * 128, :] = part.T
        half = (first_ref, second_ref)[i // (cols // 256)]
        at = i % (cols // 256) * 128
        half[:, at : at + 128] = part


def prepare(partials, gaps):
    rows, cols = partials.shape
    return pl.pallas_call(
        prepare_kernel,
        out_shape=[jax.ShapeDtypeStruct((rows, cols // 2), BF16)] * 2 + [jax.ShapeDtypeStruct((cols, rows), BF16)],
        compiler_params=pltpu.CompilerParams(vmem_limit_bytes=4 * 1024 * 1024),
        name="prepare",
    )(partials, gaps[None, :])


def table_of(e, meta_ref):
    cut = meta_ref[6]
    return jnp.where(e == 0, 3, jnp.where(e == cut, 1, jnp.where(e == cut + 1, 2, 0)))


def filter_left(raw, table, i, rows):
    white = jnp.dot(raw[i - 1], table[:rows], preferred_element_type=F32)
    white += jnp.dot(raw[i], table[rows:], preferred_element_type=F32)
    return white.astype(BF16)


def left_kernel(meta_ref, tables_ref, own, other, up_1, down_1, up_2, down_2, out_ref, raw):
    cols, rows = raw.shape[1:]
    z, yl = meta_ref[0], meta_ref[1]
    raw[4 + yl] = own[...]
    raw[5 - yl] = other[...]
    for dz, piece in ((-2, up_2), (-1, up_1), (1, down_1), (2, down_2)):
        raw[4 + 2 * dz + yl] = piece[:cols]
        raw[5 + 2 * dz - yl] = piece[cols:]
    for i in range(NE):
        e = (2 * z + i - 4) & (NE - 1)
        to = pl.ds(pl.multiple_of(e * rows, rows), rows)
        if 1 <= i < 10:
            out_ref[:, to] = filter_left(raw, tables_ref[table_of(e, meta_ref)], i, rows)
        else:
            out_ref[:, to] = jnp.zeros((cols, rows), BF16)


def right_kernel(meta_ref, tables_ref, *refs):
    pieces = refs[0:12]
    out_ref, raw = refs[12:]
    rows, half = raw.shape[2:]
    z, x, yh, core = [meta_ref[i] for i in (0, 2, 3, 4)]
    for h in range(2):
        raw[h, 0] = jnp.zeros(raw.shape[2:], BF16)

    def place(piece, b, h, dx, dy, q):
        line = NYH * ((x + dx) & 3) + (yh ^ dy)
        e = 2 * ((line - z + h * (NZ // 2)) & 7) + (core ^ q)
        raw[h, e + 1] = piece[b * rows : (b + 1) * rows]

    for q in range(2):
        for dy in range(2):
            for b in range(4):
                place(pieces[6 * q + dy], b, 0, DX[b], dy, q)
        for i in range(4):
            for dy in range(2):
                place(pieces[6 * q + 2 + i], dy, 1, DX[i], dy, q)

    @pl.loop(0, NE)
    def _(e):
        table = tables_ref[table_of(e, meta_ref)]
        for h in range(2):
            white = jnp.dot(table[:, :rows], raw[h, e], preferred_element_type=F32)
            white += jnp.dot(table[:, rows:], raw[h, e + 1], preferred_element_type=F32)
            out_ref[pl.ds(pl.multiple_of(e * rows, rows), rows), h * half : (h + 1) * half] = white.astype(BF16)


def product_kernel(scale, meta_ref, tables_ref, left_in, right_ref, up_2, down_2, up_3, down_3, far_own, far_other, out_ref, left_ref, raw):
    cols, rows = raw.shape[1:]
    z, yl = meta_ref[0], meta_ref[1]
    raw[0] = down_2[pl.ds(pl.multiple_of((1 ^ yl) * cols, cols), cols)]
    raw[7] = up_2[pl.ds(pl.multiple_of(yl * cols, cols), cols)]
    for at, piece in ((1, down_3), (5, up_3)):
        raw[at + yl] = piece[:cols]
        raw[at + 1 - yl] = piece[cols:]
    raw[3 + yl] = far_own[...]
    raw[4 - yl] = far_other[...]
    for i in range(1, 8):
        e = (2 * z + i + 5) & (NE - 1)
        to = pl.ds(pl.multiple_of(e * rows, rows), rows)
        left_ref[:, to] = filter_left(raw, tables_ref[table_of(e, meta_ref)], i, rows)
    out_ref[...] = jnp.dot(left_ref[...], right_ref[...], preferred_element_type=F32) * scale


def whitened(kernel, name, meta, tables, pieces, shape, raw_shape):
    vmem = pl.BlockSpec(memory_space=pltpu.VMEM)
    return pl.pallas_call(
        kernel,
        out_shape=jax.ShapeDtypeStruct(shape, BF16),
        in_specs=[pl.BlockSpec(memory_space=pltpu.SMEM)] + [vmem] * (1 + len(pieces)),
        out_specs=vmem,
        scratch_shapes=[pltpu.VMEM(raw_shape, BF16)],
        compiler_params=pltpu.CompilerParams(vmem_limit_bytes=16 * 1024 * 1024),
        name=name,
    )(meta, tables, *pieces)


def product(meta, tables, left, right, pieces, rows, scale):
    vmem = pl.BlockSpec(memory_space=pltpu.VMEM)
    cols = right.shape[1]
    return pl.pallas_call(
        functools.partial(product_kernel, scale),
        out_shape=[jax.ShapeDtypeStruct((cols, cols), F32), jax.ShapeDtypeStruct(left.shape, BF16)],
        in_specs=[pl.BlockSpec(memory_space=pltpu.SMEM)] + [vmem] * (3 + len(pieces)),
        out_specs=[vmem, vmem],
        scratch_shapes=[pltpu.VMEM((8, cols, rows), BF16)],
        input_output_aliases={2: 1},
        compiler_params=pltpu.CompilerParams(vmem_limit_bytes=16 * 1024 * 1024),
        name="product",
    )(meta, tables, left, right, *pieces)[0]


def on_device(partials, gaps, arc_start, taps):
    rows, cols = partials.shape
    half = cols // 2
    places = [lax.axis_index(axis) for axis in EPOCH + COL]
    meta = jnp.stack(places + [arc_start[0], arc_start[0] // rows]).astype(jnp.int32)
    a, b, own = prepare(partials, gaps)

    def up(block):
        return around(block, "z", NZ, 1)

    def down(block):
        return around(block, "z", NZ, -1)

    def along_x(block):
        return [around(block, "x", NX, step) for step in (1, -1, 2)]

    def swapped(block):
        return around(block, "c", NC, 1)

    def across(block):
        return around(block, "yh", NYH, 1)

    sync = lax.optimization_barrier
    other, up_own, down_own, a, b = sync((around(own, "yl", NYL, 1), up(own), down(own), in_plane(a, 0), in_plane(b, 1)))
    up_other, down_other, a, b, tables = sync((up(other), down(other), along_z(a, 0), along_z(b, 1), make_tables(meta, taps, rows)))
    up_1 = jnp.concatenate([up_own, up_other], axis=0)
    down_1 = jnp.concatenate([down_own, down_other], axis=0)
    up_2, down_2, a_x, b_y = sync((up(up_1), down(down_1), along_x(a), across(b)))
    a_pack = jnp.concatenate([a] + a_x, axis=0)
    b_pack = jnp.concatenate([b, b_y], axis=0)
    left = whitened(left_kernel, "left", meta, tables[1], [own, other, up_1, down_1, up_2, down_2], (cols, NE * rows), (10, cols, rows))
    up_3, down_3, a_far, b_x, left = sync((up(up_2), down(down_2), across(a_pack), along_x(b_pack), left))
    far_own, far_other = up(up_3[:cols]), down(down_3[cols:])
    mine = [a_pack, a_far, b_pack] + b_x
    theirs = [swapped(piece) for piece in mine]
    right = whitened(right_kernel, "right", meta, tables[0], mine + theirs, (NE * rows, cols), (2, NE + 1, rows, half))
    pieces = [up_2, down_2, up_3, down_3, far_own, far_other]
    return product(meta, tables[1], left, right, pieces, rows, (rows * NE) ** (-0.5))


def solution(mesh):
    fine = Mesh(mesh.devices.reshape(NZ, NYL, NX, NYH, NC), EPOCH + COL)
    in_specs = (P(EPOCH, COL), P(EPOCH), P(), P())
    return jax.shard_map(on_device, mesh=fine, in_specs=in_specs, out_specs=P(COL, EPOCH), check_vma=False)
```

```python
import functools

import jax
import jax.numpy as jnp
from jax import lax
from jax.experimental import pallas as pl
from jax.experimental.pallas import tpu as pltpu
from jax.sharding import Mesh, PartitionSpec as P

NZ, NYL, NX, NYH, NC = 8, 2, 4, 2, 2
EPOCH = ("z", "yl")
COL = ("x", "yh", "c")
NE = NZ * NYL
BF16, F32 = jnp.bfloat16, jnp.float32
DX = (0, -1, 1, 2)


def around(block, axis, n, step):
    return lax.ppermute(block, axis, [(i, (i + step) % n) for i in range(n)])


def line_of(z_from, z, half):
    return (z_from + z + half * (NZ // 2)) % NZ


def in_plane(block, half):
    axes = ("z", "yl", "x", "yh", "c")
    sizes = (NZ, NYL, NX, NYH, NC)

    def flat(place):
        index = 0
        for size, at in zip(sizes, place):
            index = index * size + at
        return index

    route = []
    for z in range(NZ):
        for yl in range(NYL):
            for x in range(NX):
                for yh in range(NYH):
                    for c in range(NC):
                        line = line_of(z, NYH * x + yh, half)
                        route.append((flat((z, yl, x, yh, c)), flat((z, c, line // NYH, line % NYH, yl))))
    return lax.ppermute(block, axes, route)


def along_z(block, half):
    route = []
    for z_from in range(NZ):
        for z in range(NZ):
            line = line_of(z_from, z, half)
            route.append(((z_from * NX + line // NYH) * NYH + line % NYH, (z * NX + line // NYH) * NYH + line % NYH))
    return lax.ppermute(block, ("z", "x", "yh"), route)


def tables_kernel(meta_ref, taps_ref, tables_ref, turned_ref):
    rows, width = tables_ref.shape[1:]
    lags = lax.broadcasted_iota(jnp.int32, (rows, width), 0)
    places = lax.broadcasted_iota(jnp.int32, (rows, width), 1)
    flip = (lags + places == rows).astype(BF16)
    flipped = jnp.dot(jnp.broadcast_to(taps_ref[...], (8, rows)), flip, preferred_element_type=F32)
    base = pltpu.roll(jnp.broadcast_to(flipped[:1], (rows, width)), 0, 1, stride=1, stride_axis=0)
    boundary = meta_ref[5]
    cut = meta_ref[6]
    for i in range(4):
        table = base
        if i == 3:
            table = jnp.where(places < rows, 0.0, base)
        elif i:
            first = (cut + i - 1) * rows
            split = (first + lags >= boundary) & (first - rows + places < boundary)
            table = jnp.where(split, 0.0, base)
        tables_ref[i] = table.astype(BF16)
        turned_ref[i] = table.T.astype(BF16)


def make_tables(meta, taps, rows):
    vmem = pl.BlockSpec(memory_space=pltpu.VMEM)
    padded = jnp.pad(taps, (0, rows - taps.shape[0]))[None, :]
    return pl.pallas_call(
        tables_kernel,
        out_shape=[jax.ShapeDtypeStruct((4, rows, 2 * rows), BF16), jax.ShapeDtypeStruct((4, 2 * rows, rows), BF16)],
        in_specs=[pl.BlockSpec(memory_space=pltpu.SMEM), vmem],
        out_specs=[vmem, vmem],
        compiler_params=pltpu.CompilerParams(vmem_limit_bytes=8 * 1024 * 1024),
        name="tables",
    )(meta, padded)


def prepare_kernel(partials_ref, gaps_ref, first_ref, second_ref, turned_ref, held, held_gaps, sems):
    rows, cols = held.shape
    copies = [pltpu.make_async_copy(gaps_ref, held_gaps, sems.at[0]), pltpu.make_async_copy(partials_ref, held, sems.at[1])]
    for copy in copies:
        copy.start()
    for copy in copies:
        copy.wait()
    kept = jnp.broadcast_to(held_gaps[...][None, :].astype(F32), (128, rows))
    kept_t = kept.T.astype(BF16)
    for i in range(cols // 128):
        part = held[:, i * 128 : (i + 1) * 128] * kept_t
        turned_ref[i * 128 : (i + 1) * 128, :] = part.T
        half = (first_ref, second_ref)[i // (cols // 256)]
        at = i % (cols // 256) * 128
        half[:, at : at + 128] = part


def prepare(partials, gaps):
    rows, cols = partials.shape
    return pl.pallas_call(
        prepare_kernel,
        out_shape=[jax.ShapeDtypeStruct((rows, cols // 2), BF16)] * 2 + [jax.ShapeDtypeStruct((cols, rows), BF16)],
        in_specs=[pl.BlockSpec(memory_space=pltpu.HBM)] * 2,
        out_specs=[pl.BlockSpec(memory_space=pltpu.VMEM)] * 3,
        scratch_shapes=[pltpu.VMEM((rows, cols), BF16), pltpu.VMEM((rows,), jnp.int32), pltpu.SemaphoreType.DMA((2,))],
        compiler_params=pltpu.CompilerParams(vmem_limit_bytes=4 * 1024 * 1024),
        name="prepare",
    )(partials, gaps)


def table_of(e, meta_ref):
    cut = meta_ref[6]
    return jnp.where(e == 0, 3, jnp.where(e == cut, 1, jnp.where(e == cut + 1, 2, 0)))


def at_block(i, rows):
    return pl.ds(pl.multiple_of(i * rows, rows), rows)


def filter_left(raw, i, e, meta_ref, tables_ref):
    rows = tables_ref.shape[2]
    table = tables_ref[table_of(e, meta_ref)]
    window = raw[:, (i - 1) * rows : (i + 1) * rows]
    return jnp.dot(window, table, preferred_element_type=F32).astype(BF16)


def left_kernel(meta_ref, tables_ref, own, other, up_1, down_1, up_2, down_2, out_ref, raw):
    cols, rows = own.shape
    z, yl = meta_ref[0], meta_ref[1]
    raw[:, at_block(4 + yl, rows)] = own[...]
    raw[:, at_block(5 - yl, rows)] = other[...]
    for dz, piece in ((-2, up_2), (-1, up_1), (1, down_1), (2, down_2)):
        raw[:, at_block(4 + 2 * dz + yl, rows)] = piece[:cols]
        raw[:, at_block(5 + 2 * dz - yl, rows)] = piece[cols:]
    for i in range(NE):
        e = (2 * z + i - 4) & (NE - 1)
        if 1 <= i < 10:
            out_ref[:, at_block(e, rows)] = filter_left(raw, i, e, meta_ref, tables_ref)
        else:
            out_ref[:, at_block(e, rows)] = jnp.zeros((cols, rows), BF16)


def right_kernel(meta_ref, tables_ref, *refs):
    pieces = refs[0:12]
    out_ref, raw = refs[12:]
    half = pieces[0].shape[1]
    rows = tables_ref.shape[1]
    z, x, yh, core = [meta_ref[i] for i in (0, 2, 3, 4)]
    raw[:rows] = jnp.zeros((rows, raw.shape[1]), BF16)

    def place(piece, b, h, dx, dy, q):
        line = NYH * ((x + dx) & 3) + (yh ^ dy)
        e = 2 * ((line - z + h * (NZ // 2)) & 7) + (core ^ q)
        raw[at_block(e + 1, rows), h * half : (h + 1) * half] = piece[b * rows : (b + 1) * rows]

    for q in range(2):
        for dy in range(2):
            for b in range(4):
                place(pieces[6 * q + dy], b, 0, DX[b], dy, q)
        for i in range(4):
            for dy in range(2):
                place(pieces[6 * q + 2 + i], dy, 1, DX[i], dy, q)
    for e in range(NE):
        table = tables_ref[table_of(e, meta_ref)]
        white = jnp.dot(table, raw[e * rows : (e + 2) * rows], preferred_element_type=F32)
        out_ref[e * rows : (e + 1) * rows] = white.astype(BF16)


def product_kernel(scale, meta_ref, tables_ref, left_in, right_ref, up_2, down_2, up_3, down_3, far_own, far_other, out_ref, left_ref, raw):
    cols, rows = far_own.shape
    z, yl = meta_ref[0], meta_ref[1]
    raw[:, :rows] = down_2[at_block(1 ^ yl, cols)]
    raw[:, 7 * rows :] = up_2[at_block(yl, cols)]
    for at, piece in ((1, down_3), (5, up_3)):
        raw[:, at_block(at + yl, rows)] = piece[:cols]
        raw[:, at_block(at + 1 - yl, rows)] = piece[cols:]
    raw[:, at_block(3 + yl, rows)] = far_own[...]
    raw[:, at_block(4 - yl, rows)] = far_other[...]
    for i in range(1, 8):
        e = (2 * z + i + 5) & (NE - 1)
        left_ref[:, at_block(e, rows)] = filter_left(raw, i, e, meta_ref, tables_ref)
    out_ref[...] = jnp.dot(left_ref[...], right_ref[...], preferred_element_type=F32) * scale


def whitened(kernel, name, meta, tables, pieces, shape, raw_shape):
    vmem = pl.BlockSpec(memory_space=pltpu.VMEM)
    return pl.pallas_call(
        kernel,
        out_shape=jax.ShapeDtypeStruct(shape, BF16),
        in_specs=[pl.BlockSpec(memory_space=pltpu.SMEM)] + [vmem] * (1 + len(pieces)),
        out_specs=vmem,
        scratch_shapes=[pltpu.VMEM(raw_shape, BF16)],
        compiler_params=pltpu.CompilerParams(vmem_limit_bytes=16 * 1024 * 1024),
        name=name,
    )(meta, tables, *pieces)


def product(meta, tables, left, right, pieces, rows, scale):
    vmem = pl.BlockSpec(memory_space=pltpu.VMEM)
    cols = right.shape[1]
    return pl.pallas_call(
        functools.partial(product_kernel, scale),
        out_shape=[jax.ShapeDtypeStruct((cols, cols), F32), jax.ShapeDtypeStruct(left.shape, BF16)],
        in_specs=[pl.BlockSpec(memory_space=pltpu.SMEM)] + [vmem] * (3 + len(pieces)),
        out_specs=[vmem, vmem],
        scratch_shapes=[pltpu.VMEM((cols, 8 * rows), BF16)],
        input_output_aliases={2: 1},
        compiler_params=pltpu.CompilerParams(vmem_limit_bytes=16 * 1024 * 1024),
        name="product",
    )(meta, tables, left, right, *pieces)[0]


def on_device(partials, gaps, arc_start, taps):
    rows, cols = partials.shape
    half = cols // 2
    places = [lax.axis_index(axis) for axis in EPOCH + COL]
    meta = jnp.stack(places + [arc_start[0], arc_start[0] // rows]).astype(jnp.int32)
    a, b, own = prepare(partials, gaps)

    def up(block):
        return around(block, "z", NZ, 1)

    def down(block):
        return around(block, "z", NZ, -1)

    def along_x(block):
        return [around(block, "x", NX, step) for step in (1, -1, 2)]

    def swapped(block):
        return around(block, "c", NC, 1)

    def across(block):
        return around(block, "yh", NYH, 1)

    sync = lax.optimization_barrier
    a, b = in_plane(a, 0), in_plane(b, 1)
    other = around(own, "yl", NYL, 1)
    up_own, down_own = up(own), down(own)
    up_own, down_own, up_other, down_other, a, b = sync((up_own, down_own, up(other), down(other), along_z(a, 0), along_z(b, 1)))
    up_1 = jnp.concatenate([up_own, up_other], axis=0)
    down_1 = jnp.concatenate([down_own, down_other], axis=0)
    tables = make_tables(meta, taps, rows)
    up_2, down_2, a_x, b_y, tables = sync((up(up_1), down(down_1), along_x(a), across(b), tables))
    a_pack = jnp.concatenate([a] + a_x, axis=0)
    b_pack = jnp.concatenate([b, b_y], axis=0)
    left = whitened(left_kernel, "left", meta, tables[1], [own, other, up_1, down_1, up_2, down_2], (cols, NE * rows), (cols, 10 * rows))
    up_3, down_3, a_far, b_x, left = sync((up(up_2), down(down_2), across(a_pack), along_x(b_pack), left))
    far_own, far_other = up(up_3[:cols]), down(down_3[cols:])
    mine = [a_pack, a_far, b_pack] + b_x
    theirs = [swapped(piece) for piece in mine]
    right = whitened(right_kernel, "right", meta, tables[0], mine + theirs, (NE * rows, cols), ((NE + 1) * rows, cols))
    pieces = [up_2, down_2, up_3, down_3, far_own, far_other]
    return product(meta, tables[1], left, right, pieces, rows, (rows * NE) ** (-0.5))


def solution(mesh):
    fine = Mesh(mesh.devices.reshape(NZ, NYL, NX, NYH, NC), EPOCH + COL)
    in_specs = (P(EPOCH, COL), P(EPOCH), P(), P())
    return jax.shard_map(on_device, mesh=fine, in_specs=in_specs, out_specs=P(COL, EPOCH), check_vma=False)
```

```python
import functools

import jax
import jax.numpy as jnp
import numpy as np
from jax import lax
from jax.experimental import pallas as pl
from jax.experimental.pallas import tpu as pltpu
from jax.sharding import Mesh, PartitionSpec as P

NZ, NYL, NX, NYH, NC = 8, 2, 4, 2, 2
EPOCH = ("z", "yl")
COL = ("x", "yh", "c")
NE = NZ * NYL
BF16, F32 = jnp.bfloat16, jnp.float32
DX = (0, -1, 1, 2)
LINE = (
    (5, 4, 7, 6, 1, 0, 2, 3),
    (0, 1, 3, 2, 4, 5, 7, 6),
    (2, 6, 5, 0, 3, 7, 1, 4),
    (3, 7, 4, 1, 2, 6, 0, 5),
    (1, 0, 6, 7, 5, 4, 3, 2),
    (4, 5, 2, 3, 0, 1, 6, 7),
    (6, 3, 1, 4, 7, 2, 5, 0),
    (7, 2, 0, 5, 6, 3, 4, 1),
)


def around(block, axis, n, step):
    return lax.ppermute(block, axis, [(i, (i + step) % n) for i in range(n)])


def in_plane(block):
    axes = ("z", "yl", "x", "yh", "c")
    sizes = (NZ, NYL, NX, NYH, NC)

    def flat(place):
        index = 0
        for size, at in zip(sizes, place):
            index = index * size + at
        return index

    route = []
    for z in range(NZ):
        for yl in range(NYL):
            for x in range(NX):
                for yh in range(NYH):
                    for c in range(NC):
                        line = LINE[z][NYH * x + yh]
                        route.append((flat((z, yl, x, yh, c)), flat((z, c, line // NYH, line % NYH, yl))))
    return lax.ppermute(block, axes, route)


def along_z(block):
    route = []
    for z_from in range(NZ):
        for z in range(NZ):
            line = LINE[z_from][z]
            route.append(((z_from * NX + line // NYH) * NYH + line % NYH, (z * NX + line // NYH) * NYH + line % NYH))
    return lax.ppermute(block, ("z", "x", "yh"), route)


def tables_kernel(meta_ref, taps_ref, tables_ref, turned_ref):
    rows, width = tables_ref.shape[1:]
    lags = lax.broadcasted_iota(jnp.int32, (rows, width), 0)
    places = lax.broadcasted_iota(jnp.int32, (rows, width), 1)
    flip = (lags + places == rows).astype(BF16)
    flipped = jnp.dot(jnp.broadcast_to(taps_ref[...], (8, rows)), flip, preferred_element_type=F32)
    base = pltpu.roll(jnp.broadcast_to(flipped[:1], (rows, width)), 0, 1, stride=1, stride_axis=0)
    boundary = meta_ref[5]
    cut = meta_ref[6]
    for i in range(4):
        table = base
        if i == 3:
            table = jnp.where(places < rows, 0.0, base)
        elif i:
            first = (cut + i - 1) * rows
            split = (first + lags >= boundary) & (first - rows + places < boundary)
            table = jnp.where(split, 0.0, base)
        tables_ref[i] = table.astype(BF16)
        turned_ref[i] = table.T.astype(BF16)


def make_tables(meta, taps, rows):
    vmem = pl.BlockSpec(memory_space=pltpu.VMEM)
    padded = jnp.pad(taps, (0, rows - taps.shape[0]))[None, :]
    return pl.pallas_call(
        tables_kernel,
        out_shape=[jax.ShapeDtypeStruct((4, rows, 2 * rows), BF16), jax.ShapeDtypeStruct((4, 2 * rows, rows), BF16)],
        in_specs=[pl.BlockSpec(memory_space=pltpu.SMEM), vmem],
        out_specs=[vmem, vmem],
        compiler_params=pltpu.CompilerParams(vmem_limit_bytes=8 * 1024 * 1024),
        name="tables",
    )(meta, padded)


def prepare_kernel(partials_ref, gaps_ref, halves_ref, turned_ref, held, held_gaps, sems):
    rows, cols = held.shape
    copies = [pltpu.make_async_copy(gaps_ref, held_gaps, sems.at[0]), pltpu.make_async_copy(partials_ref, held, sems.at[1])]
    for copy in copies:
        copy.start()
    for copy in copies:
        copy.wait()
    kept = jnp.broadcast_to(held_gaps[...][None, :].astype(F32), (128, rows))
    kept_t = kept.T.astype(BF16)
    for i in range(cols // 128):
        part = held[:, i * 128 : (i + 1) * 128] * kept_t
        turned_ref[i * 128 : (i + 1) * 128, :] = part.T
        half, at = i // (cols // 256), i % (cols // 256) * 128
        halves_ref[half * rows : (half + 1) * rows, at : at + 128] = part


def prepare(partials, gaps):
    rows, cols = partials.shape
    return pl.pallas_call(
        prepare_kernel,
        out_shape=[jax.ShapeDtypeStruct((2 * rows, cols // 2), BF16), jax.ShapeDtypeStruct((cols, rows), BF16)],
        in_specs=[pl.BlockSpec(memory_space=pltpu.HBM)] * 2,
        out_specs=[pl.BlockSpec(memory_space=pltpu.VMEM)] * 2,
        scratch_shapes=[pltpu.VMEM((rows, cols), BF16), pltpu.VMEM((rows,), jnp.int32), pltpu.SemaphoreType.DMA((2,))],
        compiler_params=pltpu.CompilerParams(vmem_limit_bytes=4 * 1024 * 1024),
        name="prepare",
    )(partials, gaps)


def table_of(e, meta_ref):
    cut = meta_ref[6]
    return jnp.where(e == 0, 3, jnp.where(e == cut, 1, jnp.where(e == cut + 1, 2, 0)))


def at_block(i, rows):
    return pl.ds(pl.multiple_of(i * rows, rows), rows)


def filter_left(raw, i, e, meta_ref, tables_ref):
    rows = tables_ref.shape[2]
    table = tables_ref[table_of(e, meta_ref)]
    window = raw[:, (i - 1) * rows : (i + 1) * rows]
    return jnp.dot(window, table, preferred_element_type=F32).astype(BF16)


def left_kernel(meta_ref, tables_ref, own, other, up_1, down_1, up_2, down_2, out_ref, raw):
    cols, rows = own.shape
    z, yl = meta_ref[0], meta_ref[1]
    raw[:, at_block(4 + yl, rows)] = own[...]
    raw[:, at_block(5 - yl, rows)] = other[...]
    for dz, piece in ((-2, up_2), (-1, up_1), (1, down_1), (2, down_2)):
        raw[:, at_block(4 + 2 * dz + yl, rows)] = piece[:cols]
        raw[:, at_block(5 + 2 * dz - yl, rows)] = piece[cols:]
    for i in range(NE):
        e = (2 * z + i - 4) & (NE - 1)
        if 1 <= i < 10:
            out_ref[:, at_block(e, rows)] = filter_left(raw, i, e, meta_ref, tables_ref)
        else:
            out_ref[:, at_block(e, rows)] = jnp.zeros((cols, rows), BF16)


def right_kernel(meta_ref, tables_ref, *refs):
    pieces = refs[0:12]
    out_ref, raw = refs[12:]
    half = pieces[0].shape[1]
    rows = tables_ref.shape[1]
    x, yh, core = [meta_ref[i] for i in (2, 3, 4)]
    raw[:rows] = jnp.zeros((rows, raw.shape[1]), BF16)

    def place(piece, b, h, dx, dy, q):
        line = NYH * ((x + dx) & 3) + (yh ^ dy)
        e = 2 * meta_ref[7 + line] + (core ^ q)
        raw[at_block(e + 1, rows), h * half : (h + 1) * half] = piece[b * rows : (b + 1) * rows]

    for q in range(2):
        for dy in range(2):
            for b in range(4):
                place(pieces[6 * q + dy], b, 0, DX[b], dy, q)
        for i in range(4):
            for dy in range(2):
                place(pieces[6 * q + 2 + i], dy, 1, DX[i], dy, q)
    for e in range(NE):
        table = tables_ref[table_of(e, meta_ref)]
        white = jnp.dot(table, raw[e * rows : (e + 2) * rows], preferred_element_type=F32)
        out_ref[e * rows : (e + 1) * rows] = white.astype(BF16)


def product_kernel(scale, meta_ref, tables_ref, left_in, right_ref, up_2, down_2, up_3, down_3, far_own, far_other, out_ref, left_ref, raw):
    cols, rows = far_own.shape
    z, yl = meta_ref[0], meta_ref[1]
    raw[:, :rows] = down_2[at_block(1 ^ yl, cols)]
    raw[:, 7 * rows :] = up_2[at_block(yl, cols)]
    for at, piece in ((1, down_3), (5, up_3)):
        raw[:, at_block(at + yl, rows)] = piece[:cols]
        raw[:, at_block(at + 1 - yl, rows)] = piece[cols:]
    raw[:, at_block(3 + yl, rows)] = far_own[...]
    raw[:, at_block(4 - yl, rows)] = far_other[...]
    for i in range(1, 8):
        e = (2 * z + i + 5) & (NE - 1)
        left_ref[:, at_block(e, rows)] = filter_left(raw, i, e, meta_ref, tables_ref)
    out_ref[...] = jnp.dot(left_ref[...], right_ref[...], preferred_element_type=F32) * scale


def whitened(kernel, name, meta, tables, pieces, shape, raw_shape):
    vmem = pl.BlockSpec(memory_space=pltpu.VMEM)
    return pl.pallas_call(
        kernel,
        out_shape=jax.ShapeDtypeStruct(shape, BF16),
        in_specs=[pl.BlockSpec(memory_space=pltpu.SMEM)] + [vmem] * (1 + len(pieces)),
        out_specs=vmem,
        scratch_shapes=[pltpu.VMEM(raw_shape, BF16)],
        compiler_params=pltpu.CompilerParams(vmem_limit_bytes=16 * 1024 * 1024),
        name=name,
    )(meta, tables, *pieces)


def product(meta, tables, left, right, pieces, rows, scale):
    vmem = pl.BlockSpec(memory_space=pltpu.VMEM)
    cols = right.shape[1]
    return pl.pallas_call(
        functools.partial(product_kernel, scale),
        out_shape=[jax.ShapeDtypeStruct((cols, cols), F32), jax.ShapeDtypeStruct(left.shape, BF16)],
        in_specs=[pl.BlockSpec(memory_space=pltpu.SMEM)] + [vmem] * (3 + len(pieces)),
        out_specs=[vmem, vmem],
        scratch_shapes=[pltpu.VMEM((cols, 8 * rows), BF16)],
        input_output_aliases={2: 1},
        compiler_params=pltpu.CompilerParams(vmem_limit_bytes=16 * 1024 * 1024),
        name="product",
    )(meta, tables, left, right, *pieces)[0]


def on_device(partials, gaps, arc_start, taps):
    rows, cols = partials.shape
    half = cols // 2
    places = [lax.axis_index(axis) for axis in EPOCH + COL]
    origin = np.argsort(np.array(LINE, np.int32), axis=0).T.astype(np.int32)
    meta = jnp.stack(places + [arc_start[0], arc_start[0] // rows]).astype(jnp.int32)
    meta = jnp.concatenate([meta, jnp.asarray(origin)[places[0]]])
    halves, own = prepare(partials, gaps)

    def up(block):
        return around(block, "z", NZ, 1)

    def down(block):
        return around(block, "z", NZ, -1)

    def along_x(block):
        return [around(block, "x", NX, step) for step in (1, -1, 2)]

    def swapped(block):
        return around(block, "c", NC, 1)

    def across(block):
        return around(block, "yh", NYH, 1)

    sync = lax.optimization_barrier
    halves = in_plane(halves)
    other = around(own, "yl", NYL, 1)
    up_own, down_own = up(own), down(own)
    up_own, down_own, up_other, down_other, halves = sync((up_own, down_own, up(other), down(other), along_z(halves)))
    a, b = halves[:rows], halves[rows:]
    up_1 = jnp.concatenate([up_own, up_other], axis=0)
    down_1 = jnp.concatenate([down_own, down_other], axis=0)
    tables = make_tables(meta, taps, rows)
    a_x, b_y, tables = sync((along_x(a), across(b), tables))
    a_pack = jnp.concatenate([a] + a_x, axis=0)
    b_pack = jnp.concatenate([b, b_y], axis=0)
    up_2, down_2, a_pack, b_pack = sync((up(up_1), down(down_1), a_pack, b_pack))
    left = whitened(left_kernel, "left", meta, tables[1], [own, other, up_1, down_1, up_2, down_2], (cols, NE * rows), (cols, 10 * rows))
    up_3, down_3, a_far, b_x, left = sync((up(up_2), down(down_2), across(a_pack), along_x(b_pack), left))
    far_own, far_other = up(up_3[:cols]), down(down_3[cols:])
    mine = [a_pack, a_far, b_pack] + b_x
    theirs = [swapped(piece) for piece in mine]
    right = whitened(right_kernel, "right", meta, tables[0], mine + theirs, (NE * rows, cols), ((NE + 1) * rows, cols))
    pieces = [up_2, down_2, up_3, down_3, far_own, far_other]
    return product(meta, tables[1], left, right, pieces, rows, (rows * NE) ** (-0.5))


def solution(mesh):
    fine = Mesh(mesh.devices.reshape(NZ, NYL, NX, NYH, NC), EPOCH + COL)
    in_specs = (P(EPOCH, COL), P(EPOCH), P(), P())
    return jax.shard_map(on_device, mesh=fine, in_specs=in_specs, out_specs=P(COL, EPOCH), check_vma=False)
```

```python
import functools

import jax
import jax.numpy as jnp
import numpy as np
from jax import lax
from jax.experimental import pallas as pl
from jax.experimental.pallas import tpu as pltpu
from jax.sharding import Mesh, PartitionSpec as P

NZ, NYL, NX, NYH, NC = 8, 2, 4, 2, 2
EPOCH = ("z", "yl")
COL = ("x", "yh", "c")
NE = NZ * NYL
BF16, F32 = jnp.bfloat16, jnp.float32
DX = (0, -1, 1, 2)
LINE = (
    (5, 4, 7, 6, 1, 0, 2, 3),
    (0, 1, 3, 2, 4, 5, 7, 6),
    (2, 6, 5, 0, 3, 7, 1, 4),
    (3, 7, 4, 1, 2, 6, 0, 5),
    (1, 0, 6, 7, 5, 4, 3, 2),
    (4, 5, 2, 3, 0, 1, 6, 7),
    (6, 3, 1, 4, 7, 2, 5, 0),
    (7, 2, 0, 5, 6, 3, 4, 1),
)


def around(block, axis, n, step):
    return lax.ppermute(block, axis, [(i, (i + step) % n) for i in range(n)])


def in_plane(block):
    axes = ("z", "yl", "x", "yh", "c")
    sizes = (NZ, NYL, NX, NYH, NC)

    def flat(place):
        index = 0
        for size, at in zip(sizes, place):
            index = index * size + at
        return index

    route = []
    for z in range(NZ):
        for yl in range(NYL):
            for x in range(NX):
                for yh in range(NYH):
                    for c in range(NC):
                        line = LINE[z][NYH * x + yh]
                        route.append((flat((z, yl, x, yh, c)), flat((z, c, line // NYH, line % NYH, yl))))
    return lax.ppermute(block, axes, route)


def along_z(block):
    route = []
    for z_from in range(NZ):
        for z in range(NZ):
            line = LINE[z_from][z]
            route.append(((z_from * NX + line // NYH) * NYH + line % NYH, (z * NX + line // NYH) * NYH + line % NYH))
    return lax.ppermute(block, ("z", "x", "yh"), route)


def tables_kernel(meta_ref, taps_ref, tables_ref, turned_ref):
    rows, width = tables_ref.shape[1:]
    lags = lax.broadcasted_iota(jnp.int32, (rows, width), 0)
    places = lax.broadcasted_iota(jnp.int32, (rows, width), 1)
    flip = (lags + places == rows).astype(BF16)
    flipped = jnp.dot(jnp.broadcast_to(taps_ref[...], (8, rows)), flip, preferred_element_type=F32)
    base = pltpu.roll(jnp.broadcast_to(flipped[:1], (rows, width)), 0, 1, stride=1, stride_axis=0)
    boundary = meta_ref[5]
    cut = meta_ref[6]
    for i in range(4):
        table = base
        if i == 3:
            table = jnp.where(places < rows, 0.0, base)
        elif i:
            first = (cut + i - 1) * rows
            split = (first + lags >= boundary) & (first - rows + places < boundary)
            table = jnp.where(split, 0.0, base)
        tables_ref[i] = table.astype(BF16)
        turned_ref[i] = table.T.astype(BF16)


def make_tables(meta, taps, rows):
    vmem = pl.BlockSpec(memory_space=pltpu.VMEM)
    padded = jnp.pad(taps, (0, rows - taps.shape[0]))[None, :]
    return pl.pallas_call(
        tables_kernel,
        out_shape=[jax.ShapeDtypeStruct((4, rows, 2 * rows), BF16), jax.ShapeDtypeStruct((4, 2 * rows, rows), BF16)],
        in_specs=[pl.BlockSpec(memory_space=pltpu.SMEM), vmem],
        out_specs=[vmem, vmem],
        compiler_params=pltpu.CompilerParams(vmem_limit_bytes=8 * 1024 * 1024),
        name="tables",
    )(meta, padded)


def prepare_kernel(partials_ref, gaps_ref, halves_ref, turned_ref, held, held_gaps, sems):
    rows, cols = held.shape
    copies = [pltpu.make_async_copy(gaps_ref, held_gaps, sems.at[0]), pltpu.make_async_copy(partials_ref, held, sems.at[1])]
    for copy in copies:
        copy.start()
    for copy in copies:
        copy.wait()
    kept = jnp.broadcast_to(held_gaps[...][None, :].astype(F32), (128, rows))
    kept_t = kept.T.astype(BF16)
    for i in range(cols // 128):
        part = held[:, i * 128 : (i + 1) * 128] * kept_t
        turned_ref[i * 128 : (i + 1) * 128, :] = part.T
        half, at = i // (cols // 256), i % (cols // 256) * 128
        halves_ref[half * rows : (half + 1) * rows, at : at + 128] = part


def prepare(partials, gaps):
    rows, cols = partials.shape
    return pl.pallas_call(
        prepare_kernel,
        out_shape=[jax.ShapeDtypeStruct((2 * rows, cols // 2), BF16), jax.ShapeDtypeStruct((cols, rows), BF16)],
        in_specs=[pl.BlockSpec(memory_space=pltpu.HBM)] * 2,
        out_specs=[pl.BlockSpec(memory_space=pltpu.VMEM)] * 2,
        scratch_shapes=[pltpu.VMEM((rows, cols), BF16), pltpu.VMEM((rows,), jnp.int32), pltpu.SemaphoreType.DMA((2,))],
        compiler_params=pltpu.CompilerParams(vmem_limit_bytes=60 * 1024 * 1024),
        name="prepare",
    )(partials, gaps)


def table_of(e, meta_ref):
    cut = meta_ref[6]
    return jnp.where(e == 0, 3, jnp.where(e == cut, 1, jnp.where(e == cut + 1, 2, 0)))


def at_block(i, rows):
    return pl.ds(pl.multiple_of(i * rows, rows), rows)


def filter_left(raw, i, e, meta_ref, tables_ref):
    rows = tables_ref.shape[2]
    table = tables_ref[table_of(e, meta_ref)]
    window = raw[:, (i - 1) * rows : (i + 1) * rows]
    return jnp.dot(window, table, preferred_element_type=F32).astype(BF16)


def left_kernel(meta_ref, tables_ref, own, other, up_1, down_1, up_2, down_2, out_ref, raw):
    cols, rows = own.shape
    z, yl = meta_ref[0], meta_ref[1]
    raw[:, at_block(4 + yl, rows)] = own[...]
    raw[:, at_block(5 - yl, rows)] = other[...]
    for dz, piece in ((-2, up_2), (-1, up_1), (1, down_1), (2, down_2)):
        raw[:, at_block(4 + 2 * dz + yl, rows)] = piece[:cols]
        raw[:, at_block(5 + 2 * dz - yl, rows)] = piece[cols:]
    for i in range(NE):
        e = (2 * z + i - 4) & (NE - 1)
        if 1 <= i < 10:
            out_ref[:, at_block(e, rows)] = filter_left(raw, i, e, meta_ref, tables_ref)
        else:
            out_ref[:, at_block(e, rows)] = jnp.zeros((cols, rows), BF16)


def right_kernel(meta_ref, tables_ref, *refs):
    pieces = refs[0:12]
    out_ref, raw = refs[12:]
    half = pieces[0].shape[1]
    rows = tables_ref.shape[1]
    z, x, yh, core = [meta_ref[i] for i in (0, 2, 3, 4)]
    raw[:rows] = jnp.zeros((rows, raw.shape[1]), BF16)

    def place(piece, b, h, dx, dy, q):
        line = NYH * ((x + dx) & 3) + (yh ^ dy)
        e = 2 * meta_ref[7 + NZ * z + line] + (core ^ q)
        raw[at_block(e + 1, rows), h * half : (h + 1) * half] = piece[b * rows : (b + 1) * rows]

    for q in range(2):
        for dy in range(2):
            for b in range(4):
                place(pieces[6 * q + dy], b, 0, DX[b], dy, q)
        for i in range(4):
            for dy in range(2):
                place(pieces[6 * q + 2 + i], dy, 1, DX[i], dy, q)
    for e in range(NE):
        table = tables_ref[table_of(e, meta_ref)]
        white = jnp.dot(table, raw[e * rows : (e + 2) * rows], preferred_element_type=F32)
        out_ref[e * rows : (e + 1) * rows] = white.astype(BF16)


def most_kernel(meta_ref, tables_ref, left_in, right_ref, up_2, down_2, up_3, down_3, out_ref, left_ref, raw):
    rows = tables_ref.shape[2]
    cols = out_ref.shape[0]
    z, yl = meta_ref[0], meta_ref[1]
    raw[:, :rows] = down_2[at_block(1 ^ yl, cols)]
    raw[:, 5 * rows :] = up_2[at_block(yl, cols)]
    for at, piece in ((1, down_3), (3, up_3)):
        raw[:, at_block(at + yl, rows)] = piece[:cols]
        raw[:, at_block(at + 1 - yl, rows)] = piece[cols:]
    for i, shift in ((1, 5), (2, 5), (4, -9), (5, -9)):
        e = (2 * z + i + shift) & (NE - 1)
        left_ref[:, at_block(e, rows)] = filter_left(raw, i, e, meta_ref, tables_ref)
    out_ref[...] = jnp.dot(left_ref[...], right_ref[...], preferred_element_type=F32)


def last_kernel(scale, meta_ref, tables_ref, most_ref, right_ref, up_3, down_3, far_own, far_other, out_ref, raw, left, right):
    cols, rows = far_own.shape
    z, yl = meta_ref[0], meta_ref[1]
    raw[:, :rows] = down_3[at_block(1 ^ yl, cols)]
    raw[:, 3 * rows :] = up_3[at_block(yl, cols)]
    raw[:, at_block(1 + yl, rows)] = far_own[...]
    raw[:, at_block(2 - yl, rows)] = far_other[...]
    for i in range(1, 4):
        e = (2 * z + i + 7) & (NE - 1)
        left[:, (i - 1) * rows : i * rows] = filter_left(raw, i, e, meta_ref, tables_ref)
        right[(i - 1) * rows : i * rows] = right_ref[at_block(e, rows)]
    out_ref[...] = (most_ref[...] + jnp.dot(left[...], right[...], preferred_element_type=F32)) * scale


def whitened(kernel, name, meta, tables, pieces, shape, raw_shape):
    vmem = pl.BlockSpec(memory_space=pltpu.VMEM)
    return pl.pallas_call(
        kernel,
        out_shape=jax.ShapeDtypeStruct(shape, BF16),
        in_specs=[pl.BlockSpec(memory_space=pltpu.SMEM)] + [vmem] * (1 + len(pieces)),
        out_specs=vmem,
        scratch_shapes=[pltpu.VMEM(raw_shape, BF16)],
        compiler_params=pltpu.CompilerParams(vmem_limit_bytes=16 * 1024 * 1024),
        name=name,
    )(meta, tables, *pieces)


def most_of_product(meta, tables, left, right, pieces, rows):
    vmem = pl.BlockSpec(memory_space=pltpu.VMEM)
    cols = right.shape[1]
    return pl.pallas_call(
        most_kernel,
        out_shape=[jax.ShapeDtypeStruct((cols, cols), F32), jax.ShapeDtypeStruct(left.shape, BF16)],
        in_specs=[pl.BlockSpec(memory_space=pltpu.SMEM)] + [vmem] * (3 + len(pieces)),
        out_specs=[vmem, vmem],
        scratch_shapes=[pltpu.VMEM((cols, 6 * rows), BF16)],
        input_output_aliases={2: 1},
        compiler_params=pltpu.CompilerParams(vmem_limit_bytes=16 * 1024 * 1024),
        name="most",
    )(meta, tables, left, right, *pieces)[0]


def product(meta, tables, most, right, pieces, rows, scale):
    vmem = pl.BlockSpec(memory_space=pltpu.VMEM)
    cols = right.shape[1]
    return pl.pallas_call(
        functools.partial(last_kernel, scale),
        out_shape=jax.ShapeDtypeStruct((cols, cols), F32),
        in_specs=[pl.BlockSpec(memory_space=pltpu.SMEM)] + [vmem] * (3 + len(pieces)),
        out_specs=vmem,
        scratch_shapes=[pltpu.VMEM((cols, 4 * rows), BF16), pltpu.VMEM((cols, 3 * rows), BF16), pltpu.VMEM((3 * rows, cols), BF16)],
        compiler_params=pltpu.CompilerParams(vmem_limit_bytes=16 * 1024 * 1024),
        name="product",
    )(meta, tables, most, right, *pieces)


def on_device(partials, gaps, arc_start, taps):
    rows, cols = partials.shape
    half = cols // 2
    places = [lax.axis_index(axis) for axis in EPOCH + COL]
    origin = np.argsort(np.array(LINE, np.int32), axis=0).T.astype(np.int32)
    meta = jnp.stack(places + [arc_start[0], arc_start[0] // rows]).astype(jnp.int32)
    meta = jnp.concatenate([meta, jnp.asarray(origin.reshape(-1))])
    halves, own = prepare(partials, gaps)

    def up(block):
        return around(block, "z", NZ, 1)

    def down(block):
        return around(block, "z", NZ, -1)

    def along_x(block):
        return [around(block, "x", NX, step) for step in (1, -1, 2)]

    def swapped(block):
        return around(block, "c", NC, 1)

    def across(block):
        return around(block, "yh", NYH, 1)

    sync = lax.optimization_barrier
    halves = in_plane(halves)
    other = around(own, "yl", NYL, 1)
    up_own, down_own = up(own), down(own)
    halves, tables = sync((halves, make_tables(meta, taps, rows)))
    up_own, down_own, up_other, down_other, halves = sync((up_own, down_own, up(other), down(other), along_z(halves)))
    a, b = halves[:rows], halves[rows:]
    up_1 = jnp.concatenate([up_own, up_other], axis=0)
    down_1 = jnp.concatenate([down_own, down_other], axis=0)
    a_x, b_y = sync((along_x(a), across(b)))
    a_pack = jnp.concatenate([a] + a_x, axis=0)
    b_pack = jnp.concatenate([b, b_y], axis=0)
    up_2, down_2, a_pack, b_pack = sync((up(up_1), down(down_1), a_pack, b_pack))
    left = whitened(left_kernel, "left", meta, tables[1], [own, other, up_1, down_1, up_2, down_2], (cols, NE * rows), (cols, 10 * rows))
    b_x = along_x(b_pack)
    early = []
    up_3, down_3, a_far, b_x, left, early = sync((up(up_2), down(down_2), across(a_pack), b_x, left, early))
    far_own, far_other = up(up_3[:cols]), down(down_3[cols:])
    mine = [a_pack, a_far, b_pack] + b_x
    theirs = [swapped(piece) for piece in mine]
    right = whitened(right_kernel, "right", meta, tables[0], mine + theirs, (NE * rows, cols), ((NE + 1) * rows, cols))
    most = most_of_product(meta, tables[1], left, right, [up_2, down_2, up_3, down_3], rows)
    return product(meta, tables[1], most, right, [up_3, down_3, far_own, far_other], rows, (rows * NE) ** (-0.5))


def solution(mesh):
    fine = Mesh(mesh.devices.reshape(NZ, NYL, NX, NYH, NC), EPOCH + COL)
    in_specs = (P(EPOCH, COL), P(EPOCH), P(), P())
    return jax.shard_map(on_device, mesh=fine, in_specs=in_specs, out_specs=P(COL, EPOCH), check_vma=False)
```

```python
import functools

import jax
import jax.numpy as jnp
import numpy as np
from jax import lax
from jax.experimental import pallas as pl
from jax.experimental.pallas import tpu as pltpu
from jax.sharding import Mesh, PartitionSpec as P

NZ, NYL, NX, NYH, NC = 8, 2, 4, 2, 2
EPOCH = ("z", "yl")
COL = ("x", "yh", "c")
NE = NZ * NYL
BF16, F32 = jnp.bfloat16, jnp.float32
DX = (0, -1, 1, 2)
LINE = (
    (5, 4, 7, 6, 1, 0, 2, 3),
    (0, 1, 3, 2, 4, 5, 7, 6),
    (2, 6, 5, 0, 3, 7, 1, 4),
    (3, 7, 4, 1, 2, 6, 0, 5),
    (1, 0, 6, 7, 5, 4, 3, 2),
    (4, 5, 2, 3, 0, 1, 6, 7),
    (6, 3, 1, 4, 7, 2, 5, 0),
    (7, 2, 0, 5, 6, 3, 4, 1),
)


def around(block, axis, n, step):
    return lax.ppermute(block, axis, [(i, (i + step) % n) for i in range(n)])


def in_plane(block):
    axes = ("z", "yl", "x", "yh", "c")
    sizes = (NZ, NYL, NX, NYH, NC)

    def flat(place):
        index = 0
        for size, at in zip(sizes, place):
            index = index * size + at
        return index

    route = []
    for z in range(NZ):
        for yl in range(NYL):
            for x in range(NX):
                for yh in range(NYH):
                    for c in range(NC):
                        line = LINE[z][NYH * x + yh]
                        route.append((flat((z, yl, x, yh, c)), flat((z, c, line // NYH, line % NYH, yl))))
    return lax.ppermute(block, axes, route)


def along_z(block):
    route = []
    for z_from in range(NZ):
        for z in range(NZ):
            line = LINE[z_from][z]
            route.append(((z_from * NX + line // NYH) * NYH + line % NYH, (z * NX + line // NYH) * NYH + line % NYH))
    return lax.ppermute(block, ("z", "x", "yh"), route)


def tables_kernel(meta_ref, taps_ref, tables_ref, turned_ref):
    rows, width = tables_ref.shape[1:]
    lags = lax.broadcasted_iota(jnp.int32, (rows, width), 0)
    places = lax.broadcasted_iota(jnp.int32, (rows, width), 1)
    flip = (lags + places == rows).astype(BF16)
    flipped = jnp.dot(jnp.broadcast_to(taps_ref[...], (8, rows)), flip, preferred_element_type=F32)
    base = pltpu.roll(jnp.broadcast_to(flipped[:1], (rows, width)), 0, 1, stride=1, stride_axis=0)
    boundary = meta_ref[5]
    cut = meta_ref[6]
    for i in range(4):
        table = base
        if i == 3:
            table = jnp.where(places < rows, 0.0, base)
        elif i:
            first = (cut + i - 1) * rows
            split = (first + lags >= boundary) & (first - rows + places < boundary)
            table = jnp.where(split, 0.0, base)
        tables_ref[i] = table.astype(BF16)
        turned_ref[i] = table.T.astype(BF16)


def make_tables(meta, taps, rows):
    vmem = pl.BlockSpec(memory_space=pltpu.VMEM)
    padded = jnp.pad(taps, (0, rows - taps.shape[0]))[None, :]
    return pl.pallas_call(
        tables_kernel,
        out_shape=[jax.ShapeDtypeStruct((4, rows, 2 * rows), BF16), jax.ShapeDtypeStruct((4, 2 * rows, rows), BF16)],
        in_specs=[pl.BlockSpec(memory_space=pltpu.SMEM), vmem],
        out_specs=[vmem, vmem],
        compiler_params=pltpu.CompilerParams(vmem_limit_bytes=8 * 1024 * 1024),
        name="tables",
    )(meta, padded)


def prepare_kernel(partials_ref, gaps_ref, halves_ref, turned_ref, held, held_gaps, sems):
    rows, cols = held.shape
    copies = [pltpu.make_async_copy(gaps_ref, held_gaps, sems.at[0]), pltpu.make_async_copy(partials_ref, held, sems.at[1])]
    for copy in copies:
        copy.start()
    for copy in copies:
        copy.wait()
    kept = jnp.broadcast_to(held_gaps[...][None, :].astype(F32), (128, rows))
    kept_t = kept.T.astype(BF16)
    for i in range(cols // 128):
        part = held[:, i * 128 : (i + 1) * 128] * kept_t
        turned_ref[i * 128 : (i + 1) * 128, :] = part.T
        half, at = i // (cols // 256), i % (cols // 256) * 128
        halves_ref[half * rows : (half + 1) * rows, at : at + 128] = part


def prepare(partials, gaps):
    rows, cols = partials.shape
    return pl.pallas_call(
        prepare_kernel,
        out_shape=[jax.ShapeDtypeStruct((2 * rows, cols // 2), BF16), jax.ShapeDtypeStruct((cols, rows), BF16)],
        in_specs=[pl.BlockSpec(memory_space=pltpu.HBM)] * 2,
        out_specs=[pl.BlockSpec(memory_space=pltpu.VMEM)] * 2,
        scratch_shapes=[pltpu.VMEM((rows, cols), BF16), pltpu.VMEM((rows,), jnp.int32), pltpu.SemaphoreType.DMA((2,))],
        compiler_params=pltpu.CompilerParams(vmem_limit_bytes=4 * 1024 * 1024),
        name="prepare",
    )(partials, gaps)


def table_of(e, meta_ref):
    cut = meta_ref[6]
    return jnp.where(e == 0, 3, jnp.where(e == cut, 1, jnp.where(e == cut + 1, 2, 0)))


def at_block(i, rows):
    return pl.ds(pl.multiple_of(i * rows, rows), rows)


def filter_left(raw, i, e, meta_ref, tables_ref):
    rows = tables_ref.shape[2]
    table = tables_ref[table_of(e, meta_ref)]
    window = raw[:, (i - 1) * rows : (i + 1) * rows]
    return jnp.dot(window, table, preferred_element_type=F32).astype(BF16)


def left_kernel(meta_ref, tables_ref, own, other, up_1, down_1, up_2, down_2, out_ref, raw):
    cols, rows = own.shape
    z, yl = meta_ref[0], meta_ref[1]
    raw[:, at_block(4 + yl, rows)] = own[...]
    raw[:, at_block(5 - yl, rows)] = other[...]
    for dz, piece in ((-2, up_2), (-1, up_1), (1, down_1), (2, down_2)):
        raw[:, at_block(4 + 2 * dz + yl, rows)] = piece[:cols]
        raw[:, at_block(5 + 2 * dz - yl, rows)] = piece[cols:]
    for i in range(NE):
        e = (2 * z + i - 4) & (NE - 1)
        if 1 <= i < 10:
            out_ref[:, at_block(e, rows)] = filter_left(raw, i, e, meta_ref, tables_ref)
        else:
            out_ref[:, at_block(e, rows)] = jnp.zeros((cols, rows), BF16)


def right_kernel(meta_ref, tables_ref, *refs):
    pieces = refs[0:12]
    out_ref, raw = refs[12:]
    half = pieces[0].shape[1]
    rows = tables_ref.shape[1]
    z, x, yh, core = [meta_ref[i] for i in (0, 2, 3, 4)]
    raw[:rows] = jnp.zeros((rows, raw.shape[1]), BF16)

    def place(piece, b, h, dx, dy, q):
        line = NYH * ((x + dx) & 3) + (yh ^ dy)
        e = 2 * meta_ref[7 + NZ * z + line] + (core ^ q)
        raw[at_block(e + 1, rows), h * half : (h + 1) * half] = piece[b * rows : (b + 1) * rows]

    for q in range(2):
        for dy in range(2):
            for b in range(4):
                place(pieces[6 * q + dy], b, 0, DX[b], dy, q)
        for i in range(4):
            for dy in range(2):
                place(pieces[6 * q + 2 + i], dy, 1, DX[i], dy, q)
    for e in range(NE):
        table = tables_ref[table_of(e, meta_ref)]
        white = jnp.dot(table, raw[e * rows : (e + 2) * rows], preferred_element_type=F32)
        out_ref[e * rows : (e + 1) * rows] = white.astype(BF16)


def most_kernel(meta_ref, tables_ref, left_in, right_ref, up_2, down_2, up_3, down_3, out_ref, left_ref, raw):
    rows = tables_ref.shape[2]
    cols = out_ref.shape[0]
    z, yl = meta_ref[0], meta_ref[1]
    raw[:, :rows] = down_2[at_block(1 ^ yl, cols)]
    raw[:, 5 * rows :] = up_2[at_block(yl, cols)]
    for at, piece in ((1, down_3), (3, up_3)):
        raw[:, at_block(at + yl, rows)] = piece[:cols]
        raw[:, at_block(at + 1 - yl, rows)] = piece[cols:]
    for i, shift in ((1, 5), (2, 5), (4, -9), (5, -9)):
        e = (2 * z + i + shift) & (NE - 1)
        left_ref[:, at_block(e, rows)] = filter_left(raw, i, e, meta_ref, tables_ref)
    out_ref[...] = jnp.dot(left_ref[...], right_ref[...], preferred_element_type=F32)


def last_kernel(scale, meta_ref, tables_ref, most_ref, right_ref, up_3, down_3, far_own, far_other, out_ref, raw, left, right):
    cols, rows = far_own.shape
    z, yl = meta_ref[0], meta_ref[1]
    raw[:, :rows] = down_3[at_block(1 ^ yl, cols)]
    raw[:, 3 * rows :] = up_3[at_block(yl, cols)]
    raw[:, at_block(1 + yl, rows)] = far_own[...]
    raw[:, at_block(2 - yl, rows)] = far_other[...]
    for i in range(1, 4):
        e = (2 * z + i + 7) & (NE - 1)
        left[:, (i - 1) * rows : i * rows] = filter_left(raw, i, e, meta_ref, tables_ref)
        right[(i - 1) * rows : i * rows] = right_ref[at_block(e, rows)]
    out_ref[...] = (most_ref[...] + jnp.dot(left[...], right[...], preferred_element_type=F32)) * scale


def whitened(kernel, name, meta, tables, pieces, shape, raw_shape):
    vmem = pl.BlockSpec(memory_space=pltpu.VMEM)
    return pl.pallas_call(
        kernel,
        out_shape=jax.ShapeDtypeStruct(shape, BF16),
        in_specs=[pl.BlockSpec(memory_space=pltpu.SMEM)] + [vmem] * (1 + len(pieces)),
        out_specs=vmem,
        scratch_shapes=[pltpu.VMEM(raw_shape, BF16)],
        compiler_params=pltpu.CompilerParams(vmem_limit_bytes=16 * 1024 * 1024),
        name=name,
    )(meta, tables, *pieces)


def most_of_product(meta, tables, left, right, pieces, rows):
    vmem = pl.BlockSpec(memory_space=pltpu.VMEM)
    cols = right.shape[1]
    return pl.pallas_call(
        most_kernel,
        out_shape=[jax.ShapeDtypeStruct((cols, cols), F32), jax.ShapeDtypeStruct(left.shape, BF16)],
        in_specs=[pl.BlockSpec(memory_space=pltpu.SMEM)] + [vmem] * (3 + len(pieces)),
        out_specs=[vmem, vmem],
        scratch_shapes=[pltpu.VMEM((cols, 6 * rows), BF16)],
        input_output_aliases={2: 1},
        compiler_params=pltpu.CompilerParams(vmem_limit_bytes=16 * 1024 * 1024),
        name="most",
    )(meta, tables, left, right, *pieces)[0]


def product(meta, tables, most, right, pieces, rows, scale):
    vmem = pl.BlockSpec(memory_space=pltpu.VMEM)
    cols = right.shape[1]
    return pl.pallas_call(
        functools.partial(last_kernel, scale),
        out_shape=jax.ShapeDtypeStruct((cols, cols), F32),
        in_specs=[pl.BlockSpec(memory_space=pltpu.SMEM)] + [vmem] * (3 + len(pieces)),
        out_specs=vmem,
        scratch_shapes=[pltpu.VMEM((cols, 4 * rows), BF16), pltpu.VMEM((cols, 3 * rows), BF16), pltpu.VMEM((3 * rows, cols), BF16)],
        compiler_params=pltpu.CompilerParams(vmem_limit_bytes=16 * 1024 * 1024),
        name="product",
    )(meta, tables, most, right, *pieces)


def on_device(partials, gaps, arc_start, taps):
    rows, cols = partials.shape
    half = cols // 2
    places = [lax.axis_index(axis) for axis in EPOCH + COL]
    origin = np.argsort(np.array(LINE, np.int32), axis=0).T.astype(np.int32)
    meta = jnp.stack(places + [arc_start[0], arc_start[0] // rows]).astype(jnp.int32)
    meta = jnp.concatenate([meta, jnp.asarray(origin.reshape(-1))])
    halves, own = prepare(partials, gaps)

    def up(block):
        return around(block, "z", NZ, 1)

    def down(block):
        return around(block, "z", NZ, -1)

    def along_x(block):
        return [around(block, "x", NX, step) for step in (1, -1, 2)]

    def swapped(block):
        return around(block, "c", NC, 1)

    def across(block):
        return around(block, "yh", NYH, 1)

    sync = lax.optimization_barrier
    halves = in_plane(halves)
    other = around(own, "yl", NYL, 1)
    up_own, down_own = up(own), down(own)
    halves, tables, up_own, down_own = sync((halves, make_tables(meta, taps, rows), up_own, down_own))
    halves = along_z(halves)
    a, b = halves[:rows], halves[rows:]
    a_x, b_y = along_x(a), across(b)
    b_pack = jnp.concatenate([b, b_y], axis=0)
    up_1 = jnp.concatenate([up_own, up(other)], axis=0)
    down_1 = jnp.concatenate([down_own, down(other)], axis=0)
    up_1, down_1, b_pack, a_x = sync((up_1, down_1, b_pack, a_x))
    a_pack = jnp.concatenate([a] + a_x, axis=0)
    up_2, down_2 = up(up_1), down(down_1)
    left = whitened(left_kernel, "left", meta, tables[1], [own, other, up_1, down_1, up_2, down_2], (cols, NE * rows), (cols, 10 * rows))
    b_x, a_far = along_x(b_pack), across(a_pack)
    up_2, down_2, b_x = sync((up_2, down_2, b_x))
    mine = [a_pack, a_far, b_pack] + b_x
    theirs = [swapped(piece) for piece in mine]
    up_3, down_3, left, theirs = sync((up(up_2), down(down_2), left, theirs))
    far_own, far_other = up(up_3[:cols]), down(down_3[cols:])
    right = whitened(right_kernel, "right", meta, tables[0], mine + theirs, (NE * rows, cols), ((NE + 1) * rows, cols))
    most = most_of_product(meta, tables[1], left, right, [up_2, down_2, up_3, down_3], rows)
    return product(meta, tables[1], most, right, [up_3, down_3, far_own, far_other], rows, (rows * NE) ** (-0.5))


def solution(mesh):
    fine = Mesh(mesh.devices.reshape(NZ, NYL, NX, NYH, NC), EPOCH + COL)
    in_specs = (P(EPOCH, COL), P(EPOCH), P(), P())
    return jax.shard_map(on_device, mesh=fine, in_specs=in_specs, out_specs=P(COL, EPOCH), check_vma=False)
```

```python
import functools

import jax
import jax.numpy as jnp
import numpy as np
from jax import lax
from jax.experimental import pallas as pl
from jax.experimental.pallas import tpu as pltpu
from jax.sharding import Mesh, PartitionSpec as P

NZ, NYL, NX, NYH, NC = 8, 2, 4, 2, 2
EPOCH = ("z", "yl")
COL = ("x", "yh", "c")
NE = NZ * NYL
BF16, F32 = jnp.bfloat16, jnp.float32
DX = (0, -1, 1, 2)
LINE = (
    (5, 4, 7, 6, 1, 0, 2, 3),
    (0, 1, 3, 2, 4, 5, 7, 6),
    (2, 6, 5, 0, 3, 7, 1, 4),
    (3, 7, 4, 1, 2, 6, 0, 5),
    (1, 0, 6, 7, 5, 4, 3, 2),
    (4, 5, 2, 3, 0, 1, 6, 7),
    (6, 3, 1, 4, 7, 2, 5, 0),
    (7, 2, 0, 5, 6, 3, 4, 1),
)


def around(block, axis, n, step):
    return lax.ppermute(block, axis, [(i, (i + step) % n) for i in range(n)])


def in_plane(block):
    axes = ("z", "yl", "x", "yh", "c")
    sizes = (NZ, NYL, NX, NYH, NC)

    def flat(place):
        index = 0
        for size, at in zip(sizes, place):
            index = index * size + at
        return index

    route = []
    for z in range(NZ):
        for yl in range(NYL):
            for x in range(NX):
                for yh in range(NYH):
                    for c in range(NC):
                        line = LINE[z][NYH * x + yh]
                        route.append((flat((z, yl, x, yh, c)), flat((z, c, line // NYH, line % NYH, yl))))
    return lax.ppermute(block, axes, route)


def along_z(block):
    route = []
    for z_from in range(NZ):
        for z in range(NZ):
            line = LINE[z_from][z]
            route.append(((z_from * NX + line // NYH) * NYH + line % NYH, (z * NX + line // NYH) * NYH + line % NYH))
    return lax.ppermute(block, ("z", "x", "yh"), route)


def tables_kernel(meta_ref, taps_ref, tables_ref, turned_ref):
    rows, width = tables_ref.shape[1:]
    lags = lax.broadcasted_iota(jnp.int32, (rows, width), 0)
    places = lax.broadcasted_iota(jnp.int32, (rows, width), 1)
    flip = (lags + places == rows).astype(BF16)
    flipped = jnp.dot(jnp.broadcast_to(taps_ref[...], (8, rows)), flip, preferred_element_type=F32)
    base = pltpu.roll(jnp.broadcast_to(flipped[:1], (rows, width)), 0, 1, stride=1, stride_axis=0)
    boundary = meta_ref[5]
    cut = meta_ref[6]
    for i in range(4):
        table = base
        if i == 3:
            table = jnp.where(places < rows, 0.0, base)
        elif i:
            first = (cut + i - 1) * rows
            split = (first + lags >= boundary) & (first - rows + places < boundary)
            table = jnp.where(split, 0.0, base)
        tables_ref[i] = table.astype(BF16)
        turned_ref[i] = table.T.astype(BF16)


def make_tables(meta, taps, rows):
    vmem = pl.BlockSpec(memory_space=pltpu.VMEM)
    padded = jnp.pad(taps, (0, rows - taps.shape[0]))[None, :]
    return pl.pallas_call(
        tables_kernel,
        out_shape=[jax.ShapeDtypeStruct((4, rows, 2 * rows), BF16), jax.ShapeDtypeStruct((4, 2 * rows, rows), BF16)],
        in_specs=[pl.BlockSpec(memory_space=pltpu.SMEM), vmem],
        out_specs=[vmem, vmem],
        compiler_params=pltpu.CompilerParams(vmem_limit_bytes=8 * 1024 * 1024),
        name="tables",
    )(meta, padded)


def prepare_kernel(partials_ref, gaps_ref, masked_ref, turned_ref, held, held_gaps, sems):
    rows, cols = held.shape
    copies = [pltpu.make_async_copy(gaps_ref, held_gaps, sems.at[0]), pltpu.make_async_copy(partials_ref, held, sems.at[1])]
    for copy in copies:
        copy.start()
    for copy in copies:
        copy.wait()
    kept = jnp.broadcast_to(held_gaps[...][None, :].astype(F32), (128, rows))
    kept_t = kept.T.astype(BF16)
    for i in range(cols // 128):
        part = held[:, i * 128 : (i + 1) * 128] * kept_t
        turned_ref[i * 128 : (i + 1) * 128, :] = part.T
        masked_ref[:, i * 128 : (i + 1) * 128] = part


def prepare(partials, gaps):
    rows, cols = partials.shape
    return pl.pallas_call(
        prepare_kernel,
        out_shape=[jax.ShapeDtypeStruct((rows, cols), BF16), jax.ShapeDtypeStruct((cols, rows), BF16)],
        in_specs=[pl.BlockSpec(memory_space=pltpu.HBM)] * 2,
        out_specs=[pl.BlockSpec(memory_space=pltpu.VMEM)] * 2,
        scratch_shapes=[pltpu.VMEM((rows, cols), BF16), pltpu.VMEM((rows,), jnp.int32), pltpu.SemaphoreType.DMA((2,))],
        compiler_params=pltpu.CompilerParams(vmem_limit_bytes=4 * 1024 * 1024),
        name="prepare",
    )(partials, gaps)


def table_of(e, meta_ref):
    cut = meta_ref[6]
    return jnp.where(e == 0, 3, jnp.where(e == cut, 1, jnp.where(e == cut + 1, 2, 0)))


def at_block(i, rows):
    return pl.ds(pl.multiple_of(i * rows, rows), rows)


def filter_left(raw, i, e, meta_ref, tables_ref):
    rows = tables_ref.shape[2]
    table = tables_ref[table_of(e, meta_ref)]
    window = raw[:, (i - 1) * rows : (i + 1) * rows]
    return jnp.dot(window, table, preferred_element_type=F32).astype(BF16)


def left_kernel(meta_ref, tables_ref, own, other, up_1, down_1, up_2, down_2, out_ref, raw):
    cols, rows = own.shape
    z, yl = meta_ref[0], meta_ref[1]
    raw[:, at_block(4 + yl, rows)] = own[...]
    raw[:, at_block(5 - yl, rows)] = other[...]
    for dz, piece in ((-2, up_2), (-1, up_1), (1, down_1), (2, down_2)):
        raw[:, at_block(4 + 2 * dz + yl, rows)] = piece[:cols]
        raw[:, at_block(5 + 2 * dz - yl, rows)] = piece[cols:]
    for i in range(NE):
        e = (2 * z + i - 4) & (NE - 1)
        if 1 <= i < 10:
            out_ref[:, at_block(e, rows)] = filter_left(raw, i, e, meta_ref, tables_ref)
        else:
            out_ref[:, at_block(e, rows)] = jnp.zeros((cols, rows), BF16)


def right_kernel(meta_ref, tables_ref, *refs):
    pieces = refs[0:8]
    out_ref, raw = refs[8:]
    rows = tables_ref.shape[1]
    z, x, yh, core = [meta_ref[i] for i in (0, 2, 3, 4)]
    raw[:rows] = jnp.zeros((rows, raw.shape[1]), BF16)
    for q in range(2):
        for s in range(4):
            for dy in range(2):
                line = NYH * ((x + DX[s]) & 3) + (yh ^ dy)
                e = 2 * meta_ref[7 + NZ * z + line] + (core ^ q)
                raw[at_block(e + 1, rows)] = pieces[4 * q + s][dy * rows : (dy + 1) * rows]
    for e in range(NE):
        table = tables_ref[table_of(e, meta_ref)]
        white = jnp.dot(table, raw[e * rows : (e + 2) * rows], preferred_element_type=F32)
        out_ref[e * rows : (e + 1) * rows] = white.astype(BF16)


def most_kernel(meta_ref, tables_ref, left_in, right_ref, up_2, down_2, up_3, down_3, out_ref, left_ref, raw):
    rows = tables_ref.shape[2]
    cols = out_ref.shape[0]
    z, yl = meta_ref[0], meta_ref[1]
    raw[:, :rows] = down_2[at_block(1 ^ yl, cols)]
    raw[:, 5 * rows :] = up_2[at_block(yl, cols)]
    for at, piece in ((1, down_3), (3, up_3)):
        raw[:, at_block(at + yl, rows)] = piece[:cols]
        raw[:, at_block(at + 1 - yl, rows)] = piece[cols:]
    for i, shift in ((1, 5), (2, 5), (4, -9), (5, -9)):
        e = (2 * z + i + shift) & (NE - 1)
        left_ref[:, at_block(e, rows)] = filter_left(raw, i, e, meta_ref, tables_ref)
    out_ref[...] = jnp.dot(left_ref[...], right_ref[...], preferred_element_type=F32)


def last_kernel(scale, meta_ref, tables_ref, most_ref, right_ref, up_3, down_3, far_own, far_other, out_ref, raw, left, right):
    cols, rows = far_own.shape
    z, yl = meta_ref[0], meta_ref[1]
    raw[:, :rows] = down_3[at_block(1 ^ yl, cols)]
    raw[:, 3 * rows :] = up_3[at_block(yl, cols)]
    raw[:, at_block(1 + yl, rows)] = far_own[...]
    raw[:, at_block(2 - yl, rows)] = far_other[...]
    for i in range(1, 4):
        e = (2 * z + i + 7) & (NE - 1)
        left[:, (i - 1) * rows : i * rows] = filter_left(raw, i, e, meta_ref, tables_ref)
        right[(i - 1) * rows : i * rows] = right_ref[at_block(e, rows)]
    out_ref[...] = (most_ref[...] + jnp.dot(left[...], right[...], preferred_element_type=F32)) * scale


def whitened(kernel, name, meta, tables, pieces, shape, raw_shape):
    vmem = pl.BlockSpec(memory_space=pltpu.VMEM)
    return pl.pallas_call(
        kernel,
        out_shape=jax.ShapeDtypeStruct(shape, BF16),
        in_specs=[pl.BlockSpec(memory_space=pltpu.SMEM)] + [vmem] * (1 + len(pieces)),
        out_specs=vmem,
        scratch_shapes=[pltpu.VMEM(raw_shape, BF16)],
        compiler_params=pltpu.CompilerParams(vmem_limit_bytes=16 * 1024 * 1024),
        name=name,
    )(meta, tables, *pieces)


def most_of_product(meta, tables, left, right, pieces, rows):
    vmem = pl.BlockSpec(memory_space=pltpu.VMEM)
    cols = right.shape[1]
    return pl.pallas_call(
        most_kernel,
        out_shape=[jax.ShapeDtypeStruct((cols, cols), F32), jax.ShapeDtypeStruct(left.shape, BF16)],
        in_specs=[pl.BlockSpec(memory_space=pltpu.SMEM)] + [vmem] * (3 + len(pieces)),
        out_specs=[vmem, vmem],
        scratch_shapes=[pltpu.VMEM((cols, 6 * rows), BF16)],
        input_output_aliases={2: 1},
        compiler_params=pltpu.CompilerParams(vmem_limit_bytes=16 * 1024 * 1024),
        name="most",
    )(meta, tables, left, right, *pieces)[0]


def product(meta, tables, most, right, pieces, rows, scale):
    vmem = pl.BlockSpec(memory_space=pltpu.VMEM)
    cols = right.shape[1]
    return pl.pallas_call(
        functools.partial(last_kernel, scale),
        out_shape=jax.ShapeDtypeStruct((cols, cols), F32),
        in_specs=[pl.BlockSpec(memory_space=pltpu.SMEM)] + [vmem] * (3 + len(pieces)),
        out_specs=vmem,
        scratch_shapes=[pltpu.VMEM((cols, 4 * rows), BF16), pltpu.VMEM((cols, 3 * rows), BF16), pltpu.VMEM((3 * rows, cols), BF16)],
        compiler_params=pltpu.CompilerParams(vmem_limit_bytes=16 * 1024 * 1024),
        name="product",
    )(meta, tables, most, right, *pieces)


def on_device(partials, gaps, arc_start, taps):
    rows, cols = partials.shape
    places = [lax.axis_index(axis) for axis in EPOCH + COL]
    origin = np.argsort(np.array(LINE, np.int32), axis=0).T.astype(np.int32)
    meta = jnp.stack(places + [arc_start[0], arc_start[0] // rows]).astype(jnp.int32)
    meta = jnp.concatenate([meta, jnp.asarray(origin.reshape(-1))])
    masked, own = prepare(partials, gaps)

    def up(block):
        return around(block, "z", NZ, 1)

    def down(block):
        return around(block, "z", NZ, -1)

    def along_x(block):
        return [around(block, "x", NX, step) for step in (1, -1, 2)]

    def swapped(block):
        return around(block, "c", NC, 1)

    def across(block):
        return around(block, "yh", NYH, 1)

    sync = lax.optimization_barrier
    here = in_plane(masked)
    other = around(own, "yl", NYL, 1)
    up_own, down_own = up(own), down(own)
    here, tables = sync((here, make_tables(meta, taps, rows)))
    up_own, down_own, up_other, down_other, here = sync((up_own, down_own, up(other), down(other), along_z(here)))
    up_1 = jnp.concatenate([up_own, up_other], axis=0)
    down_1 = jnp.concatenate([down_own, down_other], axis=0)
    pair = jnp.concatenate([here, across(here)], axis=0)
    up_2, down_2 = up(up_1), down(down_1)
    left = whitened(left_kernel, "left", meta, tables[1], [own, other, up_1, down_1, up_2, down_2], (cols, NE * rows), (cols, 10 * rows))
    mine = [pair] + along_x(pair)
    theirs = [swapped(piece) for piece in mine]
    up_3, down_3, left = sync((up(up_2), down(down_2), left))
    far_own, far_other = up(up_3[:cols]), down(down_3[cols:])
    right = whitened(right_kernel, "right", meta, tables[0], mine + theirs, (NE * rows, cols), ((NE + 1) * rows, cols))
    most = most_of_product(meta, tables[1], left, right, [up_2, down_2, up_3, down_3], rows)
    return product(meta, tables[1], most, right, [up_3, down_3, far_own, far_other], rows, (rows * NE) ** (-0.5))


def solution(mesh):
    fine = Mesh(mesh.devices.reshape(NZ, NYL, NX, NYH, NC), EPOCH + COL)
    in_specs = (P(EPOCH, COL), P(EPOCH), P(), P())
    return jax.shard_map(on_device, mesh=fine, in_specs=in_specs, out_specs=P(COL, EPOCH), check_vma=False)
```

```python
import functools

import jax
import jax.numpy as jnp
import numpy as np
from jax import lax
from jax.experimental import pallas as pl
from jax.experimental.pallas import tpu as pltpu
from jax.sharding import Mesh, PartitionSpec as P

NZ, NYL, NX, NYH, NC = 8, 2, 4, 2, 2
EPOCH = ("z", "yl")
COL = ("x", "yh", "c")
NE = NZ * NYL
BF16, F32 = jnp.bfloat16, jnp.float32
DX = (0, -1, 1, 2)
LINE = (
    (5, 4, 7, 6, 1, 0, 2, 3),
    (0, 1, 3, 2, 4, 5, 7, 6),
    (2, 6, 5, 0, 3, 7, 1, 4),
    (3, 7, 4, 1, 2, 6, 0, 5),
    (1, 0, 6, 7, 5, 4, 3, 2),
    (4, 5, 2, 3, 0, 1, 6, 7),
    (6, 3, 1, 4, 7, 2, 5, 0),
    (7, 2, 0, 5, 6, 3, 4, 1),
)


def around(block, axis, n, step):
    return lax.ppermute(block, axis, [(i, (i + step) % n) for i in range(n)])


def in_plane(block):
    axes = ("z", "yl", "x", "yh", "c")
    sizes = (NZ, NYL, NX, NYH, NC)

    def flat(place):
        index = 0
        for size, at in zip(sizes, place):
            index = index * size + at
        return index

    route = []
    for z in range(NZ):
        for yl in range(NYL):
            for x in range(NX):
                for yh in range(NYH):
                    for c in range(NC):
                        line = LINE[z][NYH * x + yh]
                        route.append((flat((z, yl, x, yh, c)), flat((z, c, line // NYH, line % NYH, yl))))
    return lax.ppermute(block, axes, route)


def along_z(block):
    route = []
    for z_from in range(NZ):
        for z in range(NZ):
            line = LINE[z_from][z]
            route.append(((z_from * NX + line // NYH) * NYH + line % NYH, (z * NX + line // NYH) * NYH + line % NYH))
    return lax.ppermute(block, ("z", "x", "yh"), route)


def tables_kernel(meta_ref, taps_ref, tables_ref, turned_ref):
    rows, width = tables_ref.shape[1:]
    lags = lax.broadcasted_iota(jnp.int32, (rows, width), 0)
    places = lax.broadcasted_iota(jnp.int32, (rows, width), 1)
    flip = (lags + places == rows).astype(BF16)
    flipped = jnp.dot(jnp.broadcast_to(taps_ref[...], (8, rows)), flip, preferred_element_type=F32)
    base = pltpu.roll(jnp.broadcast_to(flipped[:1], (rows, width)), 0, 1, stride=1, stride_axis=0)
    boundary = meta_ref[5]
    cut = meta_ref[6]
    for i in range(4):
        table = base
        if i == 3:
            table = jnp.where(places < rows, 0.0, base)
        elif i:
            first = (cut + i - 1) * rows
            split = (first + lags >= boundary) & (first - rows + places < boundary)
            table = jnp.where(split, 0.0, base)
        tables_ref[i] = table.astype(BF16)
        turned_ref[i] = table.T.astype(BF16)


def make_tables(meta, taps, rows):
    vmem = pl.BlockSpec(memory_space=pltpu.VMEM)
    padded = jnp.pad(taps, (0, rows - taps.shape[0]))[None, :]
    return pl.pallas_call(
        tables_kernel,
        out_shape=[jax.ShapeDtypeStruct((4, rows, 2 * rows), BF16), jax.ShapeDtypeStruct((4, 2 * rows, rows), BF16)],
        in_specs=[pl.BlockSpec(memory_space=pltpu.SMEM), vmem],
        out_specs=[vmem, vmem],
        compiler_params=pltpu.CompilerParams(vmem_limit_bytes=8 * 1024 * 1024),
        name="tables",
    )(meta, padded)


def prepare_kernel(partials_ref, gaps_ref, masked_ref, turned_ref, held, held_gaps, sems):
    rows, cols = held.shape
    copies = [pltpu.make_async_copy(gaps_ref, held_gaps, sems.at[0]), pltpu.make_async_copy(partials_ref, held, sems.at[1])]
    for copy in copies:
        copy.start()
    for copy in copies:
        copy.wait()
    kept = jnp.broadcast_to(held_gaps[...][None, :].astype(F32), (128, rows))
    kept_t = kept.T.astype(BF16)
    for i in range(cols // 128):
        part = held[:, i * 128 : (i + 1) * 128] * kept_t
        turned_ref[i * 128 : (i + 1) * 128, :] = part.T
        masked_ref[:, i * 128 : (i + 1) * 128] = part


def prepare(partials, gaps):
    rows, cols = partials.shape
    return pl.pallas_call(
        prepare_kernel,
        out_shape=[jax.ShapeDtypeStruct((rows, cols), BF16), jax.ShapeDtypeStruct((cols, rows), BF16)],
        in_specs=[pl.BlockSpec(memory_space=pltpu.HBM)] * 2,
        out_specs=[pl.BlockSpec(memory_space=pltpu.VMEM)] * 2,
        scratch_shapes=[pltpu.VMEM((rows, cols), BF16), pltpu.VMEM((rows,), jnp.int32), pltpu.SemaphoreType.DMA((2,))],
        compiler_params=pltpu.CompilerParams(vmem_limit_bytes=4 * 1024 * 1024),
        name="prepare",
    )(partials, gaps)


def table_of(e, meta_ref):
    cut = meta_ref[6]
    return jnp.where(e == 0, 3, jnp.where(e == cut, 1, jnp.where(e == cut + 1, 2, 0)))


def at_block(i, rows):
    return pl.ds(pl.multiple_of(i * rows, rows), rows)


def filter_left(raw, i, e, meta_ref, tables_ref):
    rows = tables_ref.shape[2]
    table = tables_ref[table_of(e, meta_ref)]
    window = raw[:, (i - 1) * rows : (i + 1) * rows]
    return jnp.dot(window, table, preferred_element_type=F32).astype(BF16)


def left_kernel(meta_ref, tables_ref, own, other, up_1, down_1, up_2, down_2, out_ref, raw):
    cols, rows = own.shape
    z, yl = meta_ref[0], meta_ref[1]
    raw[:, at_block(4 + yl, rows)] = own[...]
    raw[:, at_block(5 - yl, rows)] = other[...]
    for dz, piece in ((-2, up_2), (-1, up_1), (1, down_1), (2, down_2)):
        raw[:, at_block(4 + 2 * dz + yl, rows)] = piece[:cols]
        raw[:, at_block(5 + 2 * dz - yl, rows)] = piece[cols:]
    for i in range(NE):
        e = (2 * z + i - 4) & (NE - 1)
        if 1 <= i < 10:
            out_ref[:, at_block(e, rows)] = filter_left(raw, i, e, meta_ref, tables_ref)
        else:
            out_ref[:, at_block(e, rows)] = jnp.zeros((cols, rows), BF16)


def right_kernel(meta_ref, tables_ref, *refs):
    pieces = refs[0:8]
    out_ref, raw = refs[8:]
    rows = tables_ref.shape[1]
    z, x, yh, core = [meta_ref[i] for i in (0, 2, 3, 4)]
    raw[:rows] = jnp.zeros((rows, raw.shape[1]), BF16)
    for q in range(2):
        for s in range(4):
            for dy in range(2):
                line = NYH * ((x + DX[s]) & 3) + (yh ^ dy)
                e = 2 * meta_ref[7 + NZ * z + line] + (core ^ q)
                raw[at_block(e + 1, rows)] = pieces[4 * q + s][dy * rows : (dy + 1) * rows]
    for e in range(NE):
        table = tables_ref[table_of(e, meta_ref)]
        white = jnp.dot(table, raw[e * rows : (e + 2) * rows], preferred_element_type=F32)
        out_ref[e * rows : (e + 1) * rows] = white.astype(BF16)


def most_kernel(meta_ref, tables_ref, left_in, right_ref, up_2, down_2, up_3, down_3, out_ref, left_ref, raw):
    rows = tables_ref.shape[2]
    cols = out_ref.shape[0]
    z, yl = meta_ref[0], meta_ref[1]
    raw[:, :rows] = down_2[at_block(1 ^ yl, cols)]
    raw[:, 5 * rows :] = up_2[at_block(yl, cols)]
    for at, piece in ((1, down_3), (3, up_3)):
        raw[:, at_block(at + yl, rows)] = piece[:cols]
        raw[:, at_block(at + 1 - yl, rows)] = piece[cols:]
    for i, shift in ((1, 5), (2, 5), (4, -9), (5, -9)):
        e = (2 * z + i + shift) & (NE - 1)
        left_ref[:, at_block(e, rows)] = filter_left(raw, i, e, meta_ref, tables_ref)
    out_ref[...] = jnp.dot(left_ref[...], right_ref[...], preferred_element_type=F32)


def last_kernel(scale, meta_ref, tables_ref, most_ref, right_ref, up_3, down_3, far_own, far_other, out_ref, raw, left, right):
    cols, rows = far_own.shape
    z, yl = meta_ref[0], meta_ref[1]
    raw[:, :rows] = down_3[at_block(1 ^ yl, cols)]
    raw[:, 3 * rows :] = up_3[at_block(yl, cols)]
    raw[:, at_block(1 + yl, rows)] = far_own[...]
    raw[:, at_block(2 - yl, rows)] = far_other[...]
    for i in range(1, 4):
        e = (2 * z + i + 7) & (NE - 1)
        left[:, (i - 1) * rows : i * rows] = filter_left(raw, i, e, meta_ref, tables_ref)
        right[(i - 1) * rows : i * rows] = right_ref[at_block(e, rows)]
    out_ref[...] = (most_ref[...] + jnp.dot(left[...], right[...], preferred_element_type=F32)) * scale


def whitened(kernel, name, meta, tables, pieces, shape, raw_shape):
    vmem = pl.BlockSpec(memory_space=pltpu.VMEM)
    return pl.pallas_call(
        kernel,
        out_shape=jax.ShapeDtypeStruct(shape, BF16),
        in_specs=[pl.BlockSpec(memory_space=pltpu.SMEM)] + [vmem] * (1 + len(pieces)),
        out_specs=vmem,
        scratch_shapes=[pltpu.VMEM(raw_shape, BF16)],
        compiler_params=pltpu.CompilerParams(vmem_limit_bytes=16 * 1024 * 1024),
        name=name,
    )(meta, tables, *pieces)


def most_of_product(meta, tables, left, right, pieces, rows):
    vmem = pl.BlockSpec(memory_space=pltpu.VMEM)
    cols = right.shape[1]
    return pl.pallas_call(
        most_kernel,
        out_shape=[jax.ShapeDtypeStruct((cols, cols), F32), jax.ShapeDtypeStruct(left.shape, BF16)],
        in_specs=[pl.BlockSpec(memory_space=pltpu.SMEM)] + [vmem] * (3 + len(pieces)),
        out_specs=[vmem, vmem],
        scratch_shapes=[pltpu.VMEM((cols, 6 * rows), BF16)],
        input_output_aliases={2: 1},
        compiler_params=pltpu.CompilerParams(vmem_limit_bytes=16 * 1024 * 1024),
        name="most",
    )(meta, tables, left, right, *pieces)[0]


def product(meta, tables, most, right, pieces, rows, scale):
    vmem = pl.BlockSpec(memory_space=pltpu.VMEM)
    cols = right.shape[1]
    return pl.pallas_call(
        functools.partial(last_kernel, scale),
        out_shape=jax.ShapeDtypeStruct((cols, cols), F32),
        in_specs=[pl.BlockSpec(memory_space=pltpu.SMEM)] + [vmem] * (3 + len(pieces)),
        out_specs=vmem,
        scratch_shapes=[pltpu.VMEM((cols, 4 * rows), BF16), pltpu.VMEM((cols, 3 * rows), BF16), pltpu.VMEM((3 * rows, cols), BF16)],
        compiler_params=pltpu.CompilerParams(vmem_limit_bytes=16 * 1024 * 1024),
        name="product",
    )(meta, tables, most, right, *pieces)


def on_device(partials, gaps, arc_start, taps):
    rows, cols = partials.shape
    places = [lax.axis_index(axis) for axis in EPOCH + COL]
    origin = np.argsort(np.array(LINE, np.int32), axis=0).T.astype(np.int32)
    meta = jnp.stack(places + [arc_start[0], arc_start[0] // rows]).astype(jnp.int32)
    meta = jnp.concatenate([meta, jnp.asarray(origin.reshape(-1))])
    masked, own = prepare(partials, gaps)

    def up(block):
        return around(block, "z", NZ, 1)

    def down(block):
        return around(block, "z", NZ, -1)

    def along_x(block):
        return [around(block, "x", NX, step) for step in (1, -1, 2)]

    def swapped(block):
        return around(block, "c", NC, 1)

    def across(block):
        return around(block, "yh", NYH, 1)

    sync = lax.optimization_barrier
    here = in_plane(masked)
    other = around(own, "yl", NYL, 1)
    up_own, down_own = up(own), down(own)
    here, tables, up_own, down_own = sync((here, make_tables(meta, taps, rows), up_own, down_own))
    here = along_z(here)
    up_other, down_other = up(other), down(other)
    up_1 = jnp.concatenate([up_own, up_other], axis=0)
    down_1 = jnp.concatenate([down_own, down_other], axis=0)
    pair = jnp.concatenate([here, across(here)], axis=0)
    up_1, down_1, pair = sync((up_1, down_1, pair))
    up_2, down_2 = up(up_1), down(down_1)
    left = whitened(left_kernel, "left", meta, tables[1], [own, other, up_1, down_1, up_2, down_2], (cols, NE * rows), (cols, 10 * rows))
    mine = [pair] + along_x(pair)
    mine[3], left = sync((mine[3], left))
    up_3, down_3 = up(up_2), down(down_2)
    end_up, end_down = sync((up_3[:cols], down_3[cols:]))
    theirs = [swapped(piece) for piece in mine]
    far_own, far_other = up(end_up), down(end_down)
    right = whitened(right_kernel, "right", meta, tables[0], mine + theirs, (NE * rows, cols), ((NE + 1) * rows, cols))
    most = most_of_product(meta, tables[1], left, right, [up_2, down_2, up_3, down_3], rows)
    return product(meta, tables[1], most, right, [up_3, down_3, far_own, far_other], rows, (rows * NE) ** (-0.5))


def solution(mesh):
    fine = Mesh(mesh.devices.reshape(NZ, NYL, NX, NYH, NC), EPOCH + COL)
    in_specs = (P(EPOCH, COL), P(EPOCH), P(), P())
    return jax.shard_map(on_device, mesh=fine, in_specs=in_specs, out_specs=P(COL, EPOCH), check_vma=False)
```

```python
import functools

import jax
import jax.numpy as jnp
import numpy as np
from jax import lax
from jax.experimental import pallas as pl
from jax.experimental.pallas import tpu as pltpu
from jax.sharding import Mesh, PartitionSpec as P

NZ, NYL, NX, NYH, NC = 8, 2, 4, 2, 2
EPOCH = ("z", "yl")
COL = ("x", "yh", "c")
NE = NZ * NYL
BF16, F32 = jnp.bfloat16, jnp.float32
DX = (0, -1, 1, 2)
LINE = (
    (5, 4, 7, 6, 1, 0, 2, 3),
    (0, 1, 3, 2, 4, 5, 7, 6),
    (2, 6, 5, 0, 3, 7, 1, 4),
    (3, 7, 4, 1, 2, 6, 0, 5),
    (1, 0, 6, 7, 5, 4, 3, 2),
    (4, 5, 2, 3, 0, 1, 6, 7),
    (6, 3, 1, 4, 7, 2, 5, 0),
    (7, 2, 0, 5, 6, 3, 4, 1),
)


def around(block, axis, n, step):
    return lax.ppermute(block, axis, [(i, (i + step) % n) for i in range(n)])


def in_plane(block):
    axes = ("z", "yl", "x", "yh", "c")
    sizes = (NZ, NYL, NX, NYH, NC)

    def flat(place):
        index = 0
        for size, at in zip(sizes, place):
            index = index * size + at
        return index

    route = []
    for z in range(NZ):
        for yl in range(NYL):
            for x in range(NX):
                for yh in range(NYH):
                    for c in range(NC):
                        line = LINE[z][NYH * x + yh]
                        route.append((flat((z, yl, x, yh, c)), flat((z, c, line // NYH, line % NYH, yl))))
    return lax.ppermute(block, axes, route)


def along_z(block):
    route = []
    for z_from in range(NZ):
        for z in range(NZ):
            line = LINE[z_from][z]
            route.append(((z_from * NX + line // NYH) * NYH + line % NYH, (z * NX + line // NYH) * NYH + line % NYH))
    return lax.ppermute(block, ("z", "x", "yh"), route)


def tables_kernel(meta_ref, taps_ref, tables_ref, turned_ref):
    rows, width = tables_ref.shape[1:]
    lags = lax.broadcasted_iota(jnp.int32, (rows, width), 0)
    places = lax.broadcasted_iota(jnp.int32, (rows, width), 1)
    flip = (lags + places == rows).astype(BF16)
    flipped = jnp.dot(jnp.broadcast_to(taps_ref[...], (8, rows)), flip, preferred_element_type=F32)
    base = pltpu.roll(jnp.broadcast_to(flipped[:1], (rows, width)), 0, 1, stride=1, stride_axis=0)
    boundary = meta_ref[5]
    cut = meta_ref[6]
    for i in range(4):
        table = base
        if i == 3:
            table = jnp.where(places < rows, 0.0, base)
        elif i:
            first = (cut + i - 1) * rows
            split = (first + lags >= boundary) & (first - rows + places < boundary)
            table = jnp.where(split, 0.0, base)
        tables_ref[i] = table.astype(BF16)
        turned_ref[i] = table.T.astype(BF16)


def make_tables(meta, taps, rows):
    vmem = pl.BlockSpec(memory_space=pltpu.VMEM)
    padded = jnp.pad(taps, (0, rows - taps.shape[0]))[None, :]
    return pl.pallas_call(
        tables_kernel,
        out_shape=[jax.ShapeDtypeStruct((4, rows, 2 * rows), BF16), jax.ShapeDtypeStruct((4, 2 * rows, rows), BF16)],
        in_specs=[pl.BlockSpec(memory_space=pltpu.SMEM), vmem],
        out_specs=[vmem, vmem],
        compiler_params=pltpu.CompilerParams(vmem_limit_bytes=8 * 1024 * 1024),
        name="tables",
    )(meta, padded)


def prepare_kernel(partials_ref, gaps_ref, masked_ref, turned_ref, held, held_gaps, sems):
    rows, cols = held.shape
    copies = [pltpu.make_async_copy(gaps_ref, held_gaps, sems.at[0]), pltpu.make_async_copy(partials_ref, held, sems.at[1])]
    for copy in copies:
        copy.start()
    for copy in copies:
        copy.wait()
    kept = jnp.broadcast_to(held_gaps[...][None, :].astype(F32), (128, rows))
    kept_t = kept.T.astype(BF16)
    for i in range(cols // 128):
        part = held[:, i * 128 : (i + 1) * 128] * kept_t
        turned_ref[i * 128 : (i + 1) * 128, :] = part.T
        masked_ref[:, i * 128 : (i + 1) * 128] = part


def prepare(partials, gaps):
    rows, cols = partials.shape
    return pl.pallas_call(
        prepare_kernel,
        out_shape=[jax.ShapeDtypeStruct((rows, cols), BF16), jax.ShapeDtypeStruct((cols, rows), BF16)],
        in_specs=[pl.BlockSpec(memory_space=pltpu.HBM)] * 2,
        out_specs=[pl.BlockSpec(memory_space=pltpu.VMEM)] * 2,
        scratch_shapes=[pltpu.VMEM((rows, cols), BF16), pltpu.VMEM((rows,), jnp.int32), pltpu.SemaphoreType.DMA((2,))],
        compiler_params=pltpu.CompilerParams(vmem_limit_bytes=4 * 1024 * 1024),
        name="prepare",
    )(partials, gaps)


def table_of(e, meta_ref):
    cut = meta_ref[6]
    return jnp.where(e == 0, 3, jnp.where(e == cut, 1, jnp.where(e == cut + 1, 2, 0)))


def at_block(i, rows):
    return pl.ds(pl.multiple_of(i * rows, rows), rows)


def filter_left(raw, i, e, meta_ref, tables_ref):
    rows = tables_ref.shape[2]
    table = tables_ref[table_of(e, meta_ref)]
    window = raw[:, (i - 1) * rows : (i + 1) * rows]
    return jnp.dot(window, table, preferred_element_type=F32).astype(BF16)


def left_kernel(meta_ref, tables_ref, own, other, up_1, down_1, up_2, down_2, out_ref, raw):
    cols, rows = own.shape
    z, yl = meta_ref[0], meta_ref[1]
    raw[:, at_block(4 + yl, rows)] = own[...]
    raw[:, at_block(5 - yl, rows)] = other[...]
    for dz, piece in ((-2, up_2), (-1, up_1), (1, down_1), (2, down_2)):
        raw[:, at_block(4 + 2 * dz + yl, rows)] = piece[:cols]
        raw[:, at_block(5 + 2 * dz - yl, rows)] = piece[cols:]
    for i in range(1, 10):
        e = (2 * z + i - 4) & (NE - 1)
        out_ref[:, (i + 1) * rows : (i + 2) * rows] = filter_left(raw, i, e, meta_ref, tables_ref)


def right_kernel(meta_ref, tables_ref, *refs):
    pieces = refs[0:8]
    out_ref, raw = refs[8:]
    rows = tables_ref.shape[1]
    z, x, yh, core = [meta_ref[i] for i in (0, 2, 3, 4)]
    raw[:rows] = jnp.zeros((rows, raw.shape[1]), BF16)
    for q in range(2):
        for s in range(4):
            for dy in range(2):
                line = NYH * ((x + DX[s]) & 3) + (yh ^ dy)
                e = 2 * meta_ref[7 + NZ * z + line] + (core ^ q)
                raw[at_block(e + 1, rows)] = pieces[4 * q + s][dy * rows : (dy + 1) * rows]
    for e in range(NE):
        table = tables_ref[table_of(e, meta_ref)]
        white = jnp.dot(table, raw[e * rows : (e + 2) * rows], preferred_element_type=F32)
        out_ref[at_block((e - 2 * z + 5) & (NE - 1), rows)] = white.astype(BF16)


def most_kernel(meta_ref, tables_ref, left_in, right_ref, up_2, down_2, up_3, down_3, out_ref, left_ref, raw):
    rows = tables_ref.shape[2]
    cols = out_ref.shape[0]
    z, yl = meta_ref[0], meta_ref[1]
    raw[:, :rows] = down_2[at_block(1 ^ yl, cols)]
    raw[:, 5 * rows :] = up_2[at_block(yl, cols)]
    for at, piece in ((1, down_3), (3, up_3)):
        raw[:, at_block(at + yl, rows)] = piece[:cols]
        raw[:, at_block(at + 1 - yl, rows)] = piece[cols:]
    for i, shift in ((1, 5), (2, 5), (4, -9), (5, -9)):
        e = (2 * z + i + shift) & (NE - 1)
        at = (i + shift + 5) % NE * rows
        left_ref[:, at : at + rows] = filter_left(raw, i, e, meta_ref, tables_ref)
    depth = (NE - 3) * rows
    out_ref[...] = jnp.dot(left_ref[:, :depth], right_ref[:depth], preferred_element_type=F32)


def last_kernel(scale, meta_ref, tables_ref, most_ref, right_ref, up_3, down_3, far_own, far_other, out_ref, raw, left):
    cols, rows = far_own.shape
    z, yl = meta_ref[0], meta_ref[1]
    raw[:, :rows] = down_3[at_block(1 ^ yl, cols)]
    raw[:, 3 * rows :] = up_3[at_block(yl, cols)]
    raw[:, at_block(1 + yl, rows)] = far_own[...]
    raw[:, at_block(2 - yl, rows)] = far_other[...]
    for i in range(1, 4):
        e = (2 * z + i + 7) & (NE - 1)
        left[:, (i - 1) * rows : i * rows] = filter_left(raw, i, e, meta_ref, tables_ref)
    right = right_ref[(NE - 3) * rows :]
    out_ref[...] = (most_ref[...] + jnp.dot(left[...], right, preferred_element_type=F32)) * scale


def whitened(kernel, name, meta, tables, pieces, shape, raw_shape):
    vmem = pl.BlockSpec(memory_space=pltpu.VMEM)
    return pl.pallas_call(
        kernel,
        out_shape=jax.ShapeDtypeStruct(shape, BF16),
        in_specs=[pl.BlockSpec(memory_space=pltpu.SMEM)] + [vmem] * (1 + len(pieces)),
        out_specs=vmem,
        scratch_shapes=[pltpu.VMEM(raw_shape, BF16)],
        compiler_params=pltpu.CompilerParams(vmem_limit_bytes=16 * 1024 * 1024),
        name=name,
    )(meta, tables, *pieces)


def most_of_product(meta, tables, left, right, pieces, rows):
    vmem = pl.BlockSpec(memory_space=pltpu.VMEM)
    cols = right.shape[1]
    return pl.pallas_call(
        most_kernel,
        out_shape=[jax.ShapeDtypeStruct((cols, cols), F32), jax.ShapeDtypeStruct(left.shape, BF16)],
        in_specs=[pl.BlockSpec(memory_space=pltpu.SMEM)] + [vmem] * (3 + len(pieces)),
        out_specs=[vmem, vmem],
        scratch_shapes=[pltpu.VMEM((cols, 6 * rows), BF16)],
        input_output_aliases={2: 1},
        compiler_params=pltpu.CompilerParams(vmem_limit_bytes=16 * 1024 * 1024),
        name="most",
    )(meta, tables, left, right, *pieces)[0]


def product(meta, tables, most, right, pieces, rows, scale):
    vmem = pl.BlockSpec(memory_space=pltpu.VMEM)
    cols = right.shape[1]
    return pl.pallas_call(
        functools.partial(last_kernel, scale),
        out_shape=jax.ShapeDtypeStruct((cols, cols), F32),
        in_specs=[pl.BlockSpec(memory_space=pltpu.SMEM)] + [vmem] * (3 + len(pieces)),
        out_specs=vmem,
        scratch_shapes=[pltpu.VMEM((cols, 4 * rows), BF16), pltpu.VMEM((cols, 3 * rows), BF16)],
        compiler_params=pltpu.CompilerParams(vmem_limit_bytes=16 * 1024 * 1024),
        name="product",
    )(meta, tables, most, right, *pieces)


def on_device(partials, gaps, arc_start, taps):
    rows, cols = partials.shape
    places = [lax.axis_index(axis) for axis in EPOCH + COL]
    origin = np.argsort(np.array(LINE, np.int32), axis=0).T.astype(np.int32)
    meta = jnp.stack(places + [arc_start[0], arc_start[0] // rows]).astype(jnp.int32)
    meta = jnp.concatenate([meta, jnp.asarray(origin.reshape(-1))])
    masked, own = prepare(partials, gaps)

    def up(block):
        return around(block, "z", NZ, 1)

    def down(block):
        return around(block, "z", NZ, -1)

    def along_x(block):
        return [around(block, "x", NX, step) for step in (1, -1, 2)]

    def swapped(block):
        return around(block, "c", NC, 1)

    def across(block):
        return around(block, "yh", NYH, 1)

    sync = lax.optimization_barrier
    here = in_plane(masked)
    other = around(own, "yl", NYL, 1)
    here, tables = sync((here, make_tables(meta, taps, rows)))
    here = along_z(here)
    both = jnp.concatenate([own, other], axis=0)
    up_1, down_1 = up(both), down(both)
    pair = jnp.concatenate([here, across(here)], axis=0)
    up_1, down_1, pair = sync((up_1, down_1, pair))
    up_2, down_2 = up(up_1), down(down_1)
    left = whitened(left_kernel, "left", meta, tables[1], [own, other, up_1, down_1, up_2, down_2], (cols, NE * rows), (cols, 10 * rows))
    mine = [pair] + along_x(pair)
    mine[3], left = sync((mine[3], left))
    up_3, down_3 = up(up_2), down(down_2)
    end_up, end_down = sync((up_3[:cols], down_3[cols:]))
    theirs = [swapped(piece) for piece in mine]
    far_own, far_other = up(end_up), down(end_down)
    right = whitened(right_kernel, "right", meta, tables[0], mine + theirs, (NE * rows, cols), ((NE + 1) * rows, cols))
    most = most_of_product(meta, tables[1], left, right, [up_2, down_2, up_3, down_3], rows)
    return product(meta, tables[1], most, right, [up_3, down_3, far_own, far_other], rows, (rows * NE) ** (-0.5))


def solution(mesh):
    fine = Mesh(mesh.devices.reshape(NZ, NYL, NX, NYH, NC), EPOCH + COL)
    in_specs = (P(EPOCH, COL), P(EPOCH), P(), P())
    return jax.shard_map(on_device, mesh=fine, in_specs=in_specs, out_specs=P(COL, EPOCH), check_vma=False)
```

```python
import functools

import jax
import jax.numpy as jnp
import numpy as np
from jax import lax
from jax.experimental import pallas as pl
from jax.experimental.pallas import tpu as pltpu
from jax.sharding import Mesh, PartitionSpec as P

NZ, NYL, NX, NYH, NC = 8, 2, 4, 2, 2
EPOCH = ("z", "yl")
COL = ("x", "yh", "c")
NE = NZ * NYL
BF16, F32 = jnp.bfloat16, jnp.float32
DX = (0, -1, 1, 2)
LINE = (
    (5, 4, 7, 6, 1, 0, 2, 3),
    (0, 1, 3, 2, 4, 5, 7, 6),
    (2, 6, 5, 0, 3, 7, 1, 4),
    (3, 7, 4, 1, 2, 6, 0, 5),
    (1, 0, 6, 7, 5, 4, 3, 2),
    (4, 5, 2, 3, 0, 1, 6, 7),
    (6, 3, 1, 4, 7, 2, 5, 0),
    (7, 2, 0, 5, 6, 3, 4, 1),
)


def around(block, axis, n, step):
    return lax.ppermute(block, axis, [(i, (i + step) % n) for i in range(n)])


def in_plane(block):
    axes = ("z", "yl", "x", "yh", "c")
    sizes = (NZ, NYL, NX, NYH, NC)

    def flat(place):
        index = 0
        for size, at in zip(sizes, place):
            index = index * size + at
        return index

    route = []
    for z in range(NZ):
        for yl in range(NYL):
            for x in range(NX):
                for yh in range(NYH):
                    for c in range(NC):
                        line = LINE[z][NYH * x + yh]
                        route.append((flat((z, yl, x, yh, c)), flat((z, c, line // NYH, line % NYH, yl))))
    return lax.ppermute(block, axes, route)


def along_z(block):
    route = []
    for z_from in range(NZ):
        for z in range(NZ):
            line = LINE[z_from][z]
            route.append(((z_from * NX + line // NYH) * NYH + line % NYH, (z * NX + line // NYH) * NYH + line % NYH))
    return lax.ppermute(block, ("z", "x", "yh"), route)


def tables_kernel(meta_ref, taps_ref, tables_ref, turned_ref):
    rows, width = tables_ref.shape[1:]
    lags = lax.broadcasted_iota(jnp.int32, (rows, width), 0)
    places = lax.broadcasted_iota(jnp.int32, (rows, width), 1)
    flip = (lags + places == rows).astype(BF16)
    flipped = jnp.dot(jnp.broadcast_to(taps_ref[...], (8, rows)), flip, preferred_element_type=F32)
    base = pltpu.roll(jnp.broadcast_to(flipped[:1], (rows, width)), 0, 1, stride=1, stride_axis=0)
    boundary = meta_ref[5]
    cut = meta_ref[6]
    for i in range(4):
        table = base
        if i == 3:
            table = jnp.where(places < rows, 0.0, base)
        elif i:
            first = (cut + i - 1) * rows
            split = (first + lags >= boundary) & (first - rows + places < boundary)
            table = jnp.where(split, 0.0, base)
        tables_ref[i] = table.astype(BF16)
        turned_ref[i] = table.T.astype(BF16)


def make_tables(meta, taps, rows):
    vmem = pl.BlockSpec(memory_space=pltpu.VMEM)
    padded = jnp.pad(taps, (0, rows - taps.shape[0]))[None, :]
    return pl.pallas_call(
        tables_kernel,
        out_shape=[jax.ShapeDtypeStruct((4, rows, 2 * rows), BF16), jax.ShapeDtypeStruct((4, 2 * rows, rows), BF16)],
        in_specs=[pl.BlockSpec(memory_space=pltpu.SMEM), vmem],
        out_specs=[vmem, vmem],
        compiler_params=pltpu.CompilerParams(vmem_limit_bytes=8 * 1024 * 1024),
        name="tables",
    )(meta, padded)


def prepare_kernel(partials_ref, gaps_ref, masked_ref, turned_ref, held, held_gaps, sems):
    rows, cols = held.shape
    copies = [pltpu.make_async_copy(gaps_ref, held_gaps, sems.at[0]), pltpu.make_async_copy(partials_ref, held, sems.at[1])]
    for copy in copies:
        copy.start()
    for copy in copies:
        copy.wait()
    kept = jnp.broadcast_to(held_gaps[...][None, :].astype(F32), (128, rows))
    kept_t = kept.T.astype(BF16)
    for i in range(cols // 128):
        part = held[:, i * 128 : (i + 1) * 128] * kept_t
        turned_ref[i * 128 : (i + 1) * 128, :] = part.T
        masked_ref[:, i * 128 : (i + 1) * 128] = part


def prepare(partials, gaps):
    rows, cols = partials.shape
    return pl.pallas_call(
        prepare_kernel,
        out_shape=[jax.ShapeDtypeStruct((rows, cols), BF16), jax.ShapeDtypeStruct((cols, rows), BF16)],
        in_specs=[pl.BlockSpec(memory_space=pltpu.HBM)] * 2,
        out_specs=[pl.BlockSpec(memory_space=pltpu.VMEM)] * 2,
        scratch_shapes=[pltpu.VMEM((rows, cols), BF16), pltpu.VMEM((rows,), jnp.int32), pltpu.SemaphoreType.DMA((2,))],
        compiler_params=pltpu.CompilerParams(vmem_limit_bytes=4 * 1024 * 1024),
        name="prepare",
    )(partials, gaps)


def table_of(e, meta_ref):
    cut = meta_ref[6]
    return jnp.where(e == 0, 3, jnp.where(e == cut, 1, jnp.where(e == cut + 1, 2, 0)))


def at_block(i, rows):
    return pl.ds(pl.multiple_of(i * rows, rows), rows)


def filter_left(raw, i, e, meta_ref, tables_ref):
    rows = tables_ref.shape[2]
    table = tables_ref[table_of(e, meta_ref)]
    window = raw[:, (i - 1) * rows : (i + 1) * rows]
    return jnp.dot(window, table, preferred_element_type=F32).astype(BF16)


def left_kernel(meta_ref, tables_ref, own, other, up_1, down_1, up_2, down_2, out_ref, raw):
    cols, rows = own.shape
    z, yl = meta_ref[0], meta_ref[1]
    raw[:, at_block(4 + yl, rows)] = own[...]
    raw[:, at_block(5 - yl, rows)] = other[...]
    for dz, piece in ((-2, up_2), (-1, up_1), (1, down_1), (2, down_2)):
        raw[:, at_block(4 + 2 * dz + yl, rows)] = piece[:cols]
        raw[:, at_block(5 + 2 * dz - yl, rows)] = piece[cols:]
    for i in range(1, 10):
        e = (2 * z + i - 4) & (NE - 1)
        out_ref[:, (i + 1) * rows : (i + 2) * rows] = filter_left(raw, i, e, meta_ref, tables_ref)


def right_kernel(meta_ref, tables_ref, *refs):
    pieces = refs[0:8]
    out_ref, raw = refs[8:]
    rows = tables_ref.shape[1]
    z, x, yh, core = [meta_ref[i] for i in (0, 2, 3, 4)]
    raw[:rows] = jnp.zeros((rows, raw.shape[1]), BF16)
    for q in range(2):
        for s in range(4):
            for dy in range(2):
                line = NYH * ((x + DX[s]) & 3) + (yh ^ dy)
                e = 2 * meta_ref[7 + NZ * z + line] + (core ^ q)
                raw[at_block(e + 1, rows)] = pieces[4 * q + s][dy * rows : (dy + 1) * rows]
    for e in range(NE):
        table = tables_ref[table_of(e, meta_ref)]
        white = jnp.dot(table, raw[e * rows : (e + 2) * rows], preferred_element_type=F32)
        out_ref[at_block((e - 2 * z + 5) & (NE - 1), rows)] = white.astype(BF16)


def most_kernel(meta_ref, tables_ref, left_in, right_ref, up_2, down_2, up_3, down_3, out_ref, left_ref, raw):
    rows = tables_ref.shape[2]
    cols = out_ref.shape[0]
    z, yl = meta_ref[0], meta_ref[1]
    raw[:, :rows] = down_2[at_block(1 ^ yl, cols)]
    raw[:, 5 * rows :] = up_2[at_block(yl, cols)]
    for at, piece in ((1, down_3), (3, up_3)):
        raw[:, at_block(at + yl, rows)] = piece[:cols]
        raw[:, at_block(at + 1 - yl, rows)] = piece[cols:]
    for i, shift in ((1, 5), (2, 5), (4, -9), (5, -9)):
        e = (2 * z + i + shift) & (NE - 1)
        at = (i + shift + 5) % NE * rows
        left_ref[:, at : at + rows] = filter_left(raw, i, e, meta_ref, tables_ref)
    depth = (NE - 3) * rows
    out_ref[...] = jnp.dot(left_ref[:, :depth], right_ref[:depth], preferred_element_type=F32)


def last_kernel(scale, meta_ref, tables_ref, most_ref, right_ref, up_3, down_3, far_own, far_other, out_ref, raw, left):
    cols, rows = far_own.shape
    z, yl = meta_ref[0], meta_ref[1]
    raw[:, :rows] = down_3[at_block(1 ^ yl, cols)]
    raw[:, 3 * rows :] = up_3[at_block(yl, cols)]
    raw[:, at_block(1 + yl, rows)] = far_own[...]
    raw[:, at_block(2 - yl, rows)] = far_other[...]
    for i in range(1, 4):
        e = (2 * z + i + 7) & (NE - 1)
        left[:, (i - 1) * rows : i * rows] = filter_left(raw, i, e, meta_ref, tables_ref)
    right = right_ref[(NE - 3) * rows :]
    out_ref[...] = (most_ref[...] + jnp.dot(left[...], right, preferred_element_type=F32)) * scale


def whitened(kernel, name, meta, tables, pieces, shape, raw_shape):
    vmem = pl.BlockSpec(memory_space=pltpu.VMEM)
    return pl.pallas_call(
        kernel,
        out_shape=jax.ShapeDtypeStruct(shape, BF16),
        in_specs=[pl.BlockSpec(memory_space=pltpu.SMEM)] + [vmem] * (1 + len(pieces)),
        out_specs=vmem,
        scratch_shapes=[pltpu.VMEM(raw_shape, BF16)],
        compiler_params=pltpu.CompilerParams(vmem_limit_bytes=16 * 1024 * 1024),
        name=name,
    )(meta, tables, *pieces)


def most_of_product(meta, tables, left, right, pieces, rows):
    vmem = pl.BlockSpec(memory_space=pltpu.VMEM)
    cols = right.shape[1]
    return pl.pallas_call(
        most_kernel,
        out_shape=[jax.ShapeDtypeStruct((cols, cols), F32), jax.ShapeDtypeStruct(left.shape, BF16)],
        in_specs=[pl.BlockSpec(memory_space=pltpu.SMEM)] + [vmem] * (3 + len(pieces)),
        out_specs=[vmem, vmem],
        scratch_shapes=[pltpu.VMEM((cols, 6 * rows), BF16)],
        input_output_aliases={2: 1},
        compiler_params=pltpu.CompilerParams(vmem_limit_bytes=16 * 1024 * 1024),
        name="most",
    )(meta, tables, left, right, *pieces)[0]


def product(meta, tables, most, right, pieces, rows, scale):
    vmem = pl.BlockSpec(memory_space=pltpu.VMEM)
    cols = right.shape[1]
    return pl.pallas_call(
        functools.partial(last_kernel, scale),
        out_shape=jax.ShapeDtypeStruct((cols, cols), F32),
        in_specs=[pl.BlockSpec(memory_space=pltpu.SMEM)] + [vmem] * (3 + len(pieces)),
        out_specs=vmem,
        scratch_shapes=[pltpu.VMEM((cols, 4 * rows), BF16), pltpu.VMEM((cols, 3 * rows), BF16)],
        compiler_params=pltpu.CompilerParams(vmem_limit_bytes=16 * 1024 * 1024),
        name="product",
    )(meta, tables, most, right, *pieces)


def on_device(partials, gaps, arc_start, taps):
    rows, cols = partials.shape
    places = [lax.axis_index(axis) for axis in EPOCH + COL]
    origin = np.argsort(np.array(LINE, np.int32), axis=0).T.astype(np.int32)
    meta = jnp.stack(places + [arc_start[0], arc_start[0] // rows]).astype(jnp.int32)
    meta = jnp.concatenate([meta, jnp.asarray(origin.reshape(-1))])
    masked, own = prepare(partials, gaps)

    def up(block):
        return around(block, "z", NZ, 1)

    def down(block):
        return around(block, "z", NZ, -1)

    def along_x(block):
        return [around(block, "x", NX, step) for step in (1, -1, 2)]

    def swapped(block):
        return around(block, "c", NC, 1)

    def across(block):
        return around(block, "yh", NYH, 1)

    sync = lax.optimization_barrier
    here = in_plane(masked)
    other = around(own, "yl", NYL, 1)
    up_own, down_own = up(own), down(own)
    here, tables = sync((here, make_tables(meta, taps, rows)))
    here, up_own, down_own = sync((here, up_own, down_own))
    here = along_z(here)
    up_other, down_other = up(other), down(other)
    up_1 = jnp.concatenate([up_own, up_other], axis=0)
    down_1 = jnp.concatenate([down_own, down_other], axis=0)
    pair = jnp.concatenate([here, across(here)], axis=0)
    up_1, down_1, pair = sync((up_1, down_1, pair))
    up_2, down_2 = up(up_1), down(down_1)
    left = whitened(left_kernel, "left", meta, tables[1], [own, other, up_1, down_1, up_2, down_2], (cols, NE * rows), (cols, 10 * rows))
    mine = [pair] + along_x(pair)
    mine[3], left = sync((mine[3], left))
    up_3, down_3 = up(up_2), down(down_2)
    end_up, end_down = sync((up_3[:cols], down_3[cols:]))
    theirs = [swapped(piece) for piece in mine]
    far_own, far_other = up(end_up), down(end_down)
    right = whitened(right_kernel, "right", meta, tables[0], mine + theirs, (NE * rows, cols), ((NE + 1) * rows, cols))
    most = most_of_product(meta, tables[1], left, right, [up_2, down_2, up_3, down_3], rows)
    return product(meta, tables[1], most, right, [up_3, down_3, far_own, far_other], rows, (rows * NE) ** (-0.5))


def solution(mesh):
    fine = Mesh(mesh.devices.reshape(NZ, NYL, NX, NYH, NC), EPOCH + COL)
    in_specs = (P(EPOCH, COL), P(EPOCH), P(), P())
    return jax.shard_map(on_device, mesh=fine, in_specs=in_specs, out_specs=P(COL, EPOCH), check_vma=False)
```

```python
import functools

import jax
import jax.numpy as jnp
import numpy as np
from jax import lax
from jax.experimental import pallas as pl
from jax.experimental.pallas import tpu as pltpu
from jax.sharding import Mesh, PartitionSpec as P

NZ, NYL, NX, NYH, NC = 8, 2, 4, 2, 2
EPOCH = ("z", "yl")
COL = ("x", "yh", "c")
NE = NZ * NYL
BF16, F32 = jnp.bfloat16, jnp.float32
DX = (0, -1, 1, 2)
LINE = (
    (5, 4, 7, 6, 1, 0, 2, 3),
    (0, 1, 3, 2, 4, 5, 7, 6),
    (2, 6, 5, 0, 3, 7, 1, 4),
    (3, 7, 4, 1, 2, 6, 0, 5),
    (1, 0, 6, 7, 5, 4, 3, 2),
    (4, 5, 2, 3, 0, 1, 6, 7),
    (6, 3, 1, 4, 7, 2, 5, 0),
    (7, 2, 0, 5, 6, 3, 4, 1),
)


def around(block, axis, n, step):
    return lax.ppermute(block, axis, [(i, (i + step) % n) for i in range(n)])


def in_plane(block):
    axes = ("z", "yl", "x", "yh", "c")
    sizes = (NZ, NYL, NX, NYH, NC)

    def flat(place):
        index = 0
        for size, at in zip(sizes, place):
            index = index * size + at
        return index

    route = []
    for z in range(NZ):
        for yl in range(NYL):
            for x in range(NX):
                for yh in range(NYH):
                    for c in range(NC):
                        line = LINE[z][NYH * x + yh]
                        route.append((flat((z, yl, x, yh, c)), flat((z, c, line // NYH, line % NYH, yl))))
    return lax.ppermute(block, axes, route)


def along_z(block):
    route = []
    for z_from in range(NZ):
        for z in range(NZ):
            line = LINE[z_from][z]
            route.append(((z_from * NX + line // NYH) * NYH + line % NYH, (z * NX + line // NYH) * NYH + line % NYH))
    return lax.ppermute(block, ("z", "x", "yh"), route)


def tables_kernel(meta_ref, taps_ref, tables_ref, turned_ref):
    rows, width = tables_ref.shape[1:]
    lags = lax.broadcasted_iota(jnp.int32, (rows, width), 0)
    places = lax.broadcasted_iota(jnp.int32, (rows, width), 1)
    flip = (lags + places == rows).astype(BF16)
    flipped = jnp.dot(jnp.broadcast_to(taps_ref[...], (8, rows)), flip, preferred_element_type=F32)
    base = pltpu.roll(jnp.broadcast_to(flipped[:1], (rows, width)), 0, 1, stride=1, stride_axis=0)
    boundary = meta_ref[5]
    cut = meta_ref[6]
    for i in range(4):
        table = base
        if i == 3:
            table = jnp.where(places < rows, 0.0, base)
        elif i:
            first = (cut + i - 1) * rows
            split = (first + lags >= boundary) & (first - rows + places < boundary)
            table = jnp.where(split, 0.0, base)
        tables_ref[i] = table.astype(BF16)
        turned_ref[i] = table.T.astype(BF16)


def make_tables(meta, taps, rows):
    vmem = pl.BlockSpec(memory_space=pltpu.VMEM)
    padded = jnp.pad(taps, (0, rows - taps.shape[0]))[None, :]
    return pl.pallas_call(
        tables_kernel,
        out_shape=[jax.ShapeDtypeStruct((4, rows, 2 * rows), BF16), jax.ShapeDtypeStruct((4, 2 * rows, rows), BF16)],
        in_specs=[pl.BlockSpec(memory_space=pltpu.SMEM), vmem],
        out_specs=[vmem, vmem],
        compiler_params=pltpu.CompilerParams(vmem_limit_bytes=8 * 1024 * 1024),
        name="tables",
    )(meta, padded)


def prepare_kernel(partials_ref, gaps_ref, masked_ref, turned_ref, held, held_gaps, sems):
    rows, cols = held.shape
    copies = [pltpu.make_async_copy(gaps_ref, held_gaps, sems.at[0]), pltpu.make_async_copy(partials_ref, held, sems.at[1])]
    for copy in copies:
        copy.start()
    for copy in copies:
        copy.wait()
    kept = jnp.broadcast_to(held_gaps[...][None, :].astype(F32), (128, rows))
    kept_t = kept.T.astype(BF16)
    for i in range(cols // 128):
        part = held[:, i * 128 : (i + 1) * 128] * kept_t
        turned_ref[i * 128 : (i + 1) * 128, :] = part.T
        masked_ref[:, i * 128 : (i + 1) * 128] = part


def prepare(partials, gaps):
    rows, cols = partials.shape
    return pl.pallas_call(
        prepare_kernel,
        out_shape=[jax.ShapeDtypeStruct((rows, cols), BF16), jax.ShapeDtypeStruct((cols, rows), BF16)],
        in_specs=[pl.BlockSpec(memory_space=pltpu.HBM)] * 2,
        out_specs=[pl.BlockSpec(memory_space=pltpu.VMEM)] * 2,
        scratch_shapes=[pltpu.VMEM((rows, cols), BF16), pltpu.VMEM((rows,), jnp.int32), pltpu.SemaphoreType.DMA((2,))],
        compiler_params=pltpu.CompilerParams(vmem_limit_bytes=4 * 1024 * 1024),
        name="prepare",
    )(partials, gaps)


def table_of(e, meta_ref):
    cut = meta_ref[6]
    return jnp.where(e == 0, 3, jnp.where(e == cut, 1, jnp.where(e == cut + 1, 2, 0)))


def at_block(i, rows):
    return pl.ds(pl.multiple_of(i * rows, rows), rows)


def filter_left(raw, i, e, meta_ref, tables_ref):
    rows = tables_ref.shape[2]
    table = tables_ref[table_of(e, meta_ref)]
    window = raw[:, (i - 1) * rows : (i + 1) * rows]
    return jnp.dot(window, table, preferred_element_type=F32).astype(BF16)


def left_kernel(meta_ref, tables_ref, own, other, up_1, down_1, up_2, down_2, out_ref, raw):
    cols, rows = own.shape
    z, yl = meta_ref[0], meta_ref[1]
    raw[:, at_block(4 + yl, rows)] = own[...]
    raw[:, at_block(5 - yl, rows)] = other[...]
    for dz, piece in ((-2, up_2), (-1, up_1), (1, down_1), (2, down_2)):
        raw[:, at_block(4 + 2 * dz + yl, rows)] = piece[:cols]
        raw[:, at_block(5 + 2 * dz - yl, rows)] = piece[cols:]
    for i in range(1, 10):
        e = (2 * z + i - 4) & (NE - 1)
        out_ref[:, (i + 1) * rows : (i + 2) * rows] = filter_left(raw, i, e, meta_ref, tables_ref)


def right_kernel(meta_ref, tables_ref, *refs):
    pieces = refs[0:10]
    out_ref, raw = refs[10:]
    rows = tables_ref.shape[1]
    z, x, yh, core = [meta_ref[i] for i in (0, 2, 3, 4)]
    raw[:rows] = jnp.zeros((rows, raw.shape[1]), BF16)
    for q in range(2):
        for s in range(4):
            for dy in range(2):
                line = NYH * ((x + DX[s]) & 3) + (yh ^ dy)
                e = 2 * meta_ref[7 + NZ * z + line] + (core ^ q)
                piece, at = (pieces[5 * q + s], dy * rows) if s < 3 else (pieces[5 * q + 3 + dy], 0)
                raw[at_block(e + 1, rows)] = piece[at : at + rows]
    for e in range(NE):
        table = tables_ref[table_of(e, meta_ref)]
        white = jnp.dot(table, raw[e * rows : (e + 2) * rows], preferred_element_type=F32)
        out_ref[at_block((e - 2 * z + 5) & (NE - 1), rows)] = white.astype(BF16)


def most_kernel(meta_ref, tables_ref, left_in, right_ref, up_2, down_2, up_3, down_3, out_ref, left_ref, raw):
    rows = tables_ref.shape[2]
    cols = out_ref.shape[0]
    z, yl = meta_ref[0], meta_ref[1]
    raw[:, :rows] = down_2[at_block(1 ^ yl, cols)]
    raw[:, 5 * rows :] = up_2[at_block(yl, cols)]
    for at, piece in ((1, down_3), (3, up_3)):
        raw[:, at_block(at + yl, rows)] = piece[:cols]
        raw[:, at_block(at + 1 - yl, rows)] = piece[cols:]
    for i, shift in ((1, 5), (2, 5), (4, -9), (5, -9)):
        e = (2 * z + i + shift) & (NE - 1)
        at = (i + shift + 5) % NE * rows
        left_ref[:, at : at + rows] = filter_left(raw, i, e, meta_ref, tables_ref)
    depth = (NE - 3) * rows
    out_ref[...] = jnp.dot(left_ref[:, :depth], right_ref[:depth], preferred_element_type=F32)


def last_kernel(scale, meta_ref, tables_ref, most_ref, right_ref, up_3, down_3, far_own, far_other, out_ref, raw, left):
    cols, rows = far_own.shape
    z, yl = meta_ref[0], meta_ref[1]
    raw[:, :rows] = down_3[at_block(1 ^ yl, cols)]
    raw[:, 3 * rows :] = up_3[at_block(yl, cols)]
    raw[:, at_block(1 + yl, rows)] = far_own[...]
    raw[:, at_block(2 - yl, rows)] = far_other[...]
    for i in range(1, 4):
        e = (2 * z + i + 7) & (NE - 1)
        left[:, (i - 1) * rows : i * rows] = filter_left(raw, i, e, meta_ref, tables_ref)
    right = right_ref[(NE - 3) * rows :]
    out_ref[...] = (most_ref[...] + jnp.dot(left[...], right, preferred_element_type=F32)) * scale


def whitened(kernel, name, meta, tables, pieces, shape, raw_shape):
    vmem = pl.BlockSpec(memory_space=pltpu.VMEM)
    return pl.pallas_call(
        kernel,
        out_shape=jax.ShapeDtypeStruct(shape, BF16),
        in_specs=[pl.BlockSpec(memory_space=pltpu.SMEM)] + [vmem] * (1 + len(pieces)),
        out_specs=vmem,
        scratch_shapes=[pltpu.VMEM(raw_shape, BF16)],
        compiler_params=pltpu.CompilerParams(vmem_limit_bytes=16 * 1024 * 1024),
        name=name,
    )(meta, tables, *pieces)


def most_of_product(meta, tables, left, right, pieces, rows):
    vmem = pl.BlockSpec(memory_space=pltpu.VMEM)
    cols = right.shape[1]
    return pl.pallas_call(
        most_kernel,
        out_shape=[jax.ShapeDtypeStruct((cols, cols), F32), jax.ShapeDtypeStruct(left.shape, BF16)],
        in_specs=[pl.BlockSpec(memory_space=pltpu.SMEM)] + [vmem] * (3 + len(pieces)),
        out_specs=[vmem, vmem],
        scratch_shapes=[pltpu.VMEM((cols, 6 * rows), BF16)],
        input_output_aliases={2: 1},
        compiler_params=pltpu.CompilerParams(vmem_limit_bytes=16 * 1024 * 1024),
        name="most",
    )(meta, tables, left, right, *pieces)[0]


def product(meta, tables, most, right, pieces, rows, scale):
    vmem = pl.BlockSpec(memory_space=pltpu.VMEM)
    cols = right.shape[1]
    return pl.pallas_call(
        functools.partial(last_kernel, scale),
        out_shape=jax.ShapeDtypeStruct((cols, cols), F32),
        in_specs=[pl.BlockSpec(memory_space=pltpu.SMEM)] + [vmem] * (3 + len(pieces)),
        out_specs=vmem,
        scratch_shapes=[pltpu.VMEM((cols, 4 * rows), BF16), pltpu.VMEM((cols, 3 * rows), BF16)],
        compiler_params=pltpu.CompilerParams(vmem_limit_bytes=16 * 1024 * 1024),
        name="product",
    )(meta, tables, most, right, *pieces)


def on_device(partials, gaps, arc_start, taps):
    rows, cols = partials.shape
    places = [lax.axis_index(axis) for axis in EPOCH + COL]
    origin = np.argsort(np.array(LINE, np.int32), axis=0).T.astype(np.int32)
    meta = jnp.stack(places + [arc_start[0], arc_start[0] // rows]).astype(jnp.int32)
    meta = jnp.concatenate([meta, jnp.asarray(origin.reshape(-1))])
    masked, own = prepare(partials, gaps)

    def up(block):
        return around(block, "z", NZ, 1)

    def down(block):
        return around(block, "z", NZ, -1)

    def along_x(block):
        near = [around(block, "x", NX, step) for step in (1, -1)]
        rows = block.shape[0] // 2
        return near + [around(near[0][:rows], "x", NX, 1), around(near[1][rows:], "x", NX, -1)]

    def swapped(block):
        return around(block, "c", NC, 1)

    def across(block):
        return around(block, "yh", NYH, 1)

    sync = lax.optimization_barrier
    here = in_plane(masked)
    other = around(own, "yl", NYL, 1)
    up_own, down_own = up(own), down(own)
    here, tables = sync((here, make_tables(meta, taps, rows)))
    here, up_own, down_own = sync((here, up_own, down_own))
    here = along_z(here)
    up_other, down_other = up(other), down(other)
    up_1 = jnp.concatenate([up_own, up_other], axis=0)
    down_1 = jnp.concatenate([down_own, down_other], axis=0)
    pair = jnp.concatenate([here, across(here)], axis=0)
    up_1, down_1, pair = sync((up_1, down_1, pair))
    up_2, down_2 = up(up_1), down(down_1)
    left = whitened(left_kernel, "left", meta, tables[1], [own, other, up_1, down_1, up_2, down_2], (cols, NE * rows), (cols, 10 * rows))
    mine = [pair] + along_x(pair)
    mine[3], left = sync((mine[3], left))
    up_3, down_3 = up(up_2), down(down_2)
    end_up, end_down = sync((up_3[:cols], down_3[cols:]))
    theirs = [swapped(piece) for piece in mine]
    far_own, far_other = up(end_up), down(end_down)
    right = whitened(right_kernel, "right", meta, tables[0], mine + theirs, (NE * rows, cols), ((NE + 1) * rows, cols))
    most = most_of_product(meta, tables[1], left, right, [up_2, down_2, up_3, down_3], rows)
    return product(meta, tables[1], most, right, [up_3, down_3, far_own, far_other], rows, (rows * NE) ** (-0.5))


def solution(mesh):
    fine = Mesh(mesh.devices.reshape(NZ, NYL, NX, NYH, NC), EPOCH + COL)
    in_specs = (P(EPOCH, COL), P(EPOCH), P(), P())
    return jax.shard_map(on_device, mesh=fine, in_specs=in_specs, out_specs=P(COL, EPOCH), check_vma=False)
```

```python
import functools

import jax
import jax.numpy as jnp
import numpy as np
from jax import lax
from jax.experimental import pallas as pl
from jax.experimental.pallas import tpu as pltpu
from jax.sharding import Mesh, PartitionSpec as P

NZ, NYL, NX, NYH, NC = 8, 2, 4, 2, 2
EPOCH = ("z", "yl")
COL = ("x", "yh", "c")
NE = NZ * NYL
BF16, F32 = jnp.bfloat16, jnp.float32
DX = (0, -1, 1, 2)
LINE = (
    (5, 4, 7, 6, 1, 0, 2, 3),
    (0, 1, 3, 2, 4, 5, 7, 6),
    (2, 6, 5, 0, 3, 7, 1, 4),
    (3, 7, 4, 1, 2, 6, 0, 5),
    (1, 0, 6, 7, 5, 4, 3, 2),
    (4, 5, 2, 3, 0, 1, 6, 7),
    (6, 3, 1, 4, 7, 2, 5, 0),
    (7, 2, 0, 5, 6, 3, 4, 1),
)


def around(block, axis, n, step):
    return lax.ppermute(block, axis, [(i, (i + step) % n) for i in range(n)])


def in_plane(block):
    axes = ("z", "yl", "x", "yh", "c")
    sizes = (NZ, NYL, NX, NYH, NC)

    def flat(place):
        index = 0
        for size, at in zip(sizes, place):
            index = index * size + at
        return index

    route = []
    for z in range(NZ):
        for yl in range(NYL):
            for x in range(NX):
                for yh in range(NYH):
                    for c in range(NC):
                        line = LINE[z][NYH * x + yh]
                        route.append((flat((z, yl, x, yh, c)), flat((z, c, line // NYH, line % NYH, yl))))
    return lax.ppermute(block, axes, route)


def along_z(block):
    route = []
    for z_from in range(NZ):
        for z in range(NZ):
            line = LINE[z_from][z]
            route.append(((z_from * NX + line // NYH) * NYH + line % NYH, (z * NX + line // NYH) * NYH + line % NYH))
    return lax.ppermute(block, ("z", "x", "yh"), route)


def tables_kernel(meta_ref, taps_ref, tables_ref, turned_ref):
    rows, width = tables_ref.shape[1:]
    lags = lax.broadcasted_iota(jnp.int32, (rows, width), 0)
    places = lax.broadcasted_iota(jnp.int32, (rows, width), 1)
    flip = (lags + places == rows).astype(BF16)
    flipped = jnp.dot(jnp.broadcast_to(taps_ref[...], (8, rows)), flip, preferred_element_type=F32)
    base = pltpu.roll(jnp.broadcast_to(flipped[:1], (rows, width)), 0, 1, stride=1, stride_axis=0)
    boundary = meta_ref[5]
    cut = meta_ref[6]
    for i in range(4):
        table = base
        if i == 3:
            table = jnp.where(places < rows, 0.0, base)
        elif i:
            first = (cut + i - 1) * rows
            split = (first + lags >= boundary) & (first - rows + places < boundary)
            table = jnp.where(split, 0.0, base)
        tables_ref[i] = table.astype(BF16)
        turned_ref[i] = table.T.astype(BF16)


def make_tables(meta, taps, rows):
    vmem = pl.BlockSpec(memory_space=pltpu.VMEM)
    padded = jnp.pad(taps, (0, rows - taps.shape[0]))[None, :]
    return pl.pallas_call(
        tables_kernel,
        out_shape=[jax.ShapeDtypeStruct((4, rows, 2 * rows), BF16), jax.ShapeDtypeStruct((4, 2 * rows, rows), BF16)],
        in_specs=[pl.BlockSpec(memory_space=pltpu.SMEM), vmem],
        out_specs=[vmem, vmem],
        compiler_params=pltpu.CompilerParams(vmem_limit_bytes=8 * 1024 * 1024),
        name="tables",
    )(meta, padded)


def prepare_kernel(partials_ref, gaps_ref, masked_ref, turned_ref, held, held_gaps, sems):
    rows, cols = held.shape
    copies = [pltpu.make_async_copy(gaps_ref, held_gaps, sems.at[0]), pltpu.make_async_copy(partials_ref, held, sems.at[1])]
    for copy in copies:
        copy.start()
    for copy in copies:
        copy.wait()
    kept = jnp.broadcast_to(held_gaps[...][None, :].astype(F32), (128, rows))
    kept_t = kept.T.astype(BF16)
    for i in range(cols // 128):
        part = held[:, i * 128 : (i + 1) * 128] * kept_t
        turned_ref[i * 128 : (i + 1) * 128, :] = part.T
        masked_ref[:, i * 128 : (i + 1) * 128] = part


def prepare(partials, gaps):
    rows, cols = partials.shape
    return pl.pallas_call(
        prepare_kernel,
        out_shape=[jax.ShapeDtypeStruct((rows, cols), BF16), jax.ShapeDtypeStruct((cols, rows), BF16)],
        in_specs=[pl.BlockSpec(memory_space=pltpu.HBM)] * 2,
        out_specs=[pl.BlockSpec(memory_space=pltpu.VMEM)] * 2,
        scratch_shapes=[pltpu.VMEM((rows, cols), BF16), pltpu.VMEM((rows,), jnp.int32), pltpu.SemaphoreType.DMA((2,))],
        compiler_params=pltpu.CompilerParams(vmem_limit_bytes=4 * 1024 * 1024),
        name="prepare",
    )(partials, gaps)


def table_of(e, meta_ref):
    cut = meta_ref[6]
    return jnp.where(e == 0, 3, jnp.where(e == cut, 1, jnp.where(e == cut + 1, 2, 0)))


def at_block(i, rows):
    return pl.ds(pl.multiple_of(i * rows, rows), rows)


def filter_left(raw, i, e, meta_ref, tables_ref):
    rows = tables_ref.shape[2]
    table = tables_ref[table_of(e, meta_ref)]
    window = raw[:, (i - 1) * rows : (i + 1) * rows]
    return jnp.dot(window, table, preferred_element_type=F32).astype(BF16)


def left_kernel(meta_ref, tables_ref, own, other, up_1, down_1, up_2, down_2, out_ref, raw):
    cols, rows = own.shape
    z, yl = meta_ref[0], meta_ref[1]
    raw[:, at_block(4 + yl, rows)] = own[...]
    raw[:, at_block(5 - yl, rows)] = other[...]
    for dz, piece in ((-2, up_2), (-1, up_1), (1, down_1), (2, down_2)):
        raw[:, at_block(4 + 2 * dz + yl, rows)] = piece[:cols]
        raw[:, at_block(5 + 2 * dz - yl, rows)] = piece[cols:]
    for i in range(1, 10):
        e = (2 * z + i - 4) & (NE - 1)
        out_ref[:, (i + 1) * rows : (i + 2) * rows] = filter_left(raw, i, e, meta_ref, tables_ref)


def right_kernel(meta_ref, tables_ref, *refs):
    pieces = refs[0:10]
    out_ref, raw = refs[10:]
    rows = tables_ref.shape[1]
    z, x, yh, core = [meta_ref[i] for i in (0, 2, 3, 4)]
    raw[:rows] = jnp.zeros((rows, raw.shape[1]), BF16)
    for q in range(2):
        for s in range(4):
            for dy in range(2):
                line = NYH * ((x + DX[s]) & 3) + (yh ^ dy)
                e = 2 * meta_ref[7 + NZ * z + line] + (core ^ q)
                piece, at = (pieces[5 * q + s], dy * rows) if s < 3 else (pieces[5 * q + 3 + dy], 0)
                raw[at_block(e + 1, rows)] = piece[at : at + rows]
    for e in range(NE):
        table = tables_ref[table_of(e, meta_ref)]
        white = jnp.dot(table, raw[e * rows : (e + 2) * rows], preferred_element_type=F32)
        out_ref[at_block((e - 2 * z + 5) & (NE - 1), rows)] = white.astype(BF16)


def most_kernel(meta_ref, tables_ref, left_in, right_ref, up_2, down_2, up_3, down_3, out_ref, left_ref, raw):
    rows = tables_ref.shape[2]
    cols = out_ref.shape[0]
    z, yl = meta_ref[0], meta_ref[1]
    raw[:, :rows] = down_2[at_block(1 ^ yl, cols)]
    raw[:, 5 * rows :] = up_2[at_block(yl, cols)]
    for at, piece in ((1, down_3), (3, up_3)):
        raw[:, at_block(at + yl, rows)] = piece[:cols]
        raw[:, at_block(at + 1 - yl, rows)] = piece[cols:]
    for i, shift in ((1, 5), (2, 5), (4, -9), (5, -9)):
        e = (2 * z + i + shift) & (NE - 1)
        at = (i + shift + 5) % NE * rows
        left_ref[:, at : at + rows] = filter_left(raw, i, e, meta_ref, tables_ref)
    depth = (NE - 3) * rows
    out_ref[...] = jnp.dot(left_ref[:, :depth], right_ref[:depth], preferred_element_type=F32)


def last_kernel(scale, meta_ref, tables_ref, most_ref, right_ref, up_3, down_3, far_own, far_other, out_ref, raw, left):
    cols, rows = far_own.shape
    z, yl = meta_ref[0], meta_ref[1]
    raw[:, :rows] = down_3[at_block(1 ^ yl, cols)]
    raw[:, 3 * rows :] = up_3[at_block(yl, cols)]
    raw[:, at_block(1 + yl, rows)] = far_own[...]
    raw[:, at_block(2 - yl, rows)] = far_other[...]
    for i in range(1, 4):
        e = (2 * z + i + 7) & (NE - 1)
        left[:, (i - 1) * rows : i * rows] = filter_left(raw, i, e, meta_ref, tables_ref)
    right = right_ref[(NE - 3) * rows :]
    out_ref[...] = (most_ref[...] + jnp.dot(left[...], right, preferred_element_type=F32)) * scale


def whitened(kernel, name, meta, tables, pieces, shape, raw_shape):
    vmem = pl.BlockSpec(memory_space=pltpu.VMEM)
    return pl.pallas_call(
        kernel,
        out_shape=jax.ShapeDtypeStruct(shape, BF16),
        in_specs=[pl.BlockSpec(memory_space=pltpu.SMEM)] + [vmem] * (1 + len(pieces)),
        out_specs=vmem,
        scratch_shapes=[pltpu.VMEM(raw_shape, BF16)],
        compiler_params=pltpu.CompilerParams(vmem_limit_bytes=16 * 1024 * 1024),
        name=name,
    )(meta, tables, *pieces)


def most_of_product(meta, tables, left, right, pieces, rows):
    vmem = pl.BlockSpec(memory_space=pltpu.VMEM)
    cols = right.shape[1]
    return pl.pallas_call(
        most_kernel,
        out_shape=[jax.ShapeDtypeStruct((cols, cols), F32), jax.ShapeDtypeStruct(left.shape, BF16)],
        in_specs=[pl.BlockSpec(memory_space=pltpu.SMEM)] + [vmem] * (3 + len(pieces)),
        out_specs=[vmem, vmem],
        scratch_shapes=[pltpu.VMEM((cols, 6 * rows), BF16)],
        input_output_aliases={2: 1},
        compiler_params=pltpu.CompilerParams(vmem_limit_bytes=16 * 1024 * 1024),
        name="most",
    )(meta, tables, left, right, *pieces)[0]


def product(meta, tables, most, right, pieces, rows, scale):
    vmem = pl.BlockSpec(memory_space=pltpu.VMEM)
    cols = right.shape[1]
    return pl.pallas_call(
        functools.partial(last_kernel, scale),
        out_shape=jax.ShapeDtypeStruct((cols, cols), F32),
        in_specs=[pl.BlockSpec(memory_space=pltpu.SMEM)] + [vmem] * (3 + len(pieces)),
        out_specs=vmem,
        scratch_shapes=[pltpu.VMEM((cols, 4 * rows), BF16), pltpu.VMEM((cols, 3 * rows), BF16)],
        compiler_params=pltpu.CompilerParams(vmem_limit_bytes=16 * 1024 * 1024),
        name="product",
    )(meta, tables, most, right, *pieces)


def on_device(partials, gaps, arc_start, taps):
    rows, cols = partials.shape
    places = [lax.axis_index(axis) for axis in EPOCH + COL]
    origin = np.argsort(np.array(LINE, np.int32), axis=0).T.astype(np.int32)
    meta = jnp.stack(places + [arc_start[0], arc_start[0] // rows]).astype(jnp.int32)
    meta = jnp.concatenate([meta, jnp.asarray(origin.reshape(-1))])
    masked, own = prepare(partials, gaps)

    def up(block):
        return around(block, "z", NZ, 1)

    def down(block):
        return around(block, "z", NZ, -1)

    def along_x(block):
        near = [around(block, "x", NX, step) for step in (1, -1)]
        rows = block.shape[0] // 2
        return near + [around(near[0][:rows], "x", NX, 1), around(near[1][rows:], "x", NX, -1)]

    def swapped(block):
        return around(block, "c", NC, 1)

    def across(block):
        return around(block, "yh", NYH, 1)

    sync = lax.optimization_barrier
    here = in_plane(masked)
    other = around(own, "yl", NYL, 1)
    up_own, down_own = up(own), down(own)
    here, other, tables = sync((here, other, make_tables(meta, taps, rows)))
    here = along_z(here)
    up_own, down_own, here = sync((up_own, down_own, here))
    up_other, down_other = up(other), down(other)
    up_1 = jnp.concatenate([up_own, up_other], axis=0)
    down_1 = jnp.concatenate([down_own, down_other], axis=0)
    pair = jnp.concatenate([here, across(here)], axis=0)
    up_1, down_1, pair = sync((up_1, down_1, pair))
    up_2, down_2 = up(up_1), down(down_1)
    left = whitened(left_kernel, "left", meta, tables[1], [own, other, up_1, down_1, up_2, down_2], (cols, NE * rows), (cols, 10 * rows))
    mine = [pair] + along_x(pair)
    mine[3], left = sync((mine[3], left))
    up_3, down_3 = up(up_2), down(down_2)
    end_up, end_down = sync((up_3[:cols], down_3[cols:]))
    theirs = [swapped(piece) for piece in mine]
    far_own, far_other = up(end_up), down(end_down)
    right = whitened(right_kernel, "right", meta, tables[0], mine + theirs, (NE * rows, cols), ((NE + 1) * rows, cols))
    most = most_of_product(meta, tables[1], left, right, [up_2, down_2, up_3, down_3], rows)
    return product(meta, tables[1], most, right, [up_3, down_3, far_own, far_other], rows, (rows * NE) ** (-0.5))


def solution(mesh):
    fine = Mesh(mesh.devices.reshape(NZ, NYL, NX, NYH, NC), EPOCH + COL)
    in_specs = (P(EPOCH, COL), P(EPOCH), P(), P())
    return jax.shard_map(on_device, mesh=fine, in_specs=in_specs, out_specs=P(COL, EPOCH), check_vma=False)
```

```python
import functools

import jax
import jax.numpy as jnp
import numpy as np
from jax import lax
from jax.experimental import pallas as pl
from jax.experimental.pallas import tpu as pltpu
from jax.sharding import Mesh, PartitionSpec as P

NZ, NYL, NX, NYH, NC = 8, 2, 4, 2, 2
EPOCH = ("z", "yl")
COL = ("x", "yh", "c")
NE = NZ * NYL
BF16, F32 = jnp.bfloat16, jnp.float32
DX = (0, -1, 1, 2)
LINE = (
    (5, 4, 7, 6, 1, 0, 2, 3),
    (0, 1, 3, 2, 4, 5, 7, 6),
    (2, 6, 5, 0, 3, 7, 1, 4),
    (3, 7, 4, 1, 2, 6, 0, 5),
    (1, 0, 6, 7, 5, 4, 3, 2),
    (4, 5, 2, 3, 0, 1, 6, 7),
    (6, 3, 1, 4, 7, 2, 5, 0),
    (7, 2, 0, 5, 6, 3, 4, 1),
)


def around(block, axis, n, step):
    return lax.ppermute(block, axis, [(i, (i + step) % n) for i in range(n)])


def in_plane(block):
    axes = ("z", "yl", "x", "yh", "c")
    sizes = (NZ, NYL, NX, NYH, NC)

    def flat(place):
        index = 0
        for size, at in zip(sizes, place):
            index = index * size + at
        return index

    route = []
    for z in range(NZ):
        for yl in range(NYL):
            for x in range(NX):
                for yh in range(NYH):
                    for c in range(NC):
                        line = LINE[z][NYH * x + yh]
                        route.append((flat((z, yl, x, yh, c)), flat((z, c, line // NYH, line % NYH, yl))))
    return lax.ppermute(block, axes, route)


def along_z(block):
    route = []
    for z_from in range(NZ):
        for z in range(NZ):
            line = LINE[z_from][z]
            route.append(((z_from * NX + line // NYH) * NYH + line % NYH, (z * NX + line // NYH) * NYH + line % NYH))
    return lax.ppermute(block, ("z", "x", "yh"), route)


def tables_kernel(meta_ref, taps_ref, tables_ref, turned_ref):
    rows, width = tables_ref.shape[1:]
    lags = lax.broadcasted_iota(jnp.int32, (rows, width), 0)
    places = lax.broadcasted_iota(jnp.int32, (rows, width), 1)
    flip = (lags + places == rows).astype(BF16)
    flipped = jnp.dot(jnp.broadcast_to(taps_ref[...], (8, rows)), flip, preferred_element_type=F32)
    base = pltpu.roll(jnp.broadcast_to(flipped[:1], (rows, width)), 0, 1, stride=1, stride_axis=0)
    boundary = meta_ref[5]
    cut = meta_ref[6]
    for i in range(4):
        table = base
        if i == 3:
            table = jnp.where(places < rows, 0.0, base)
        elif i:
            first = (cut + i - 1) * rows
            split = (first + lags >= boundary) & (first - rows + places < boundary)
            table = jnp.where(split, 0.0, base)
        tables_ref[i] = table.astype(BF16)
        turned_ref[i] = table.T.astype(BF16)


def make_tables(meta, taps, rows):
    vmem = pl.BlockSpec(memory_space=pltpu.VMEM)
    padded = jnp.pad(taps, (0, rows - taps.shape[0]))[None, :]
    return pl.pallas_call(
        tables_kernel,
        out_shape=[jax.ShapeDtypeStruct((4, rows, 2 * rows), BF16), jax.ShapeDtypeStruct((4, 2 * rows, rows), BF16)],
        in_specs=[pl.BlockSpec(memory_space=pltpu.SMEM), vmem],
        out_specs=[vmem, vmem],
        compiler_params=pltpu.CompilerParams(vmem_limit_bytes=8 * 1024 * 1024),
        name="tables",
    )(meta, padded)


def prepare_kernel(partials_ref, gaps_ref, masked_ref, turned_ref, held, held_gaps, sems):
    rows, cols = held.shape
    copies = [pltpu.make_async_copy(gaps_ref, held_gaps, sems.at[0]), pltpu.make_async_copy(partials_ref, held, sems.at[1])]
    for copy in copies:
        copy.start()
    for copy in copies:
        copy.wait()
    kept = jnp.broadcast_to(held_gaps[...][None, :].astype(F32), (128, rows))
    kept_t = kept.T.astype(BF16)
    for i in range(cols // 128):
        part = held[:, i * 128 : (i + 1) * 128] * kept_t
        turned_ref[i * 128 : (i + 1) * 128, :] = part.T
        masked_ref[:, i * 128 : (i + 1) * 128] = part


def prepare(partials, gaps):
    rows, cols = partials.shape
    return pl.pallas_call(
        prepare_kernel,
        out_shape=[jax.ShapeDtypeStruct((rows, cols), BF16), jax.ShapeDtypeStruct((cols, rows), BF16)],
        in_specs=[pl.BlockSpec(memory_space=pltpu.HBM)] * 2,
        out_specs=[pl.BlockSpec(memory_space=pltpu.VMEM)] * 2,
        scratch_shapes=[pltpu.VMEM((rows, cols), BF16), pltpu.VMEM((rows,), jnp.int32), pltpu.SemaphoreType.DMA((2,))],
        compiler_params=pltpu.CompilerParams(vmem_limit_bytes=4 * 1024 * 1024),
        name="prepare",
    )(partials, gaps)


def table_of(e, meta_ref):
    cut = meta_ref[6]
    return jnp.where(e == 0, 3, jnp.where(e == cut, 1, jnp.where(e == cut + 1, 2, 0)))


def at_block(i, rows):
    return pl.ds(pl.multiple_of(i * rows, rows), rows)


def filter_left(raw, i, e, meta_ref, tables_ref):
    rows = tables_ref.shape[2]
    table = tables_ref[table_of(e, meta_ref)]
    window = raw[:, (i - 1) * rows : (i + 1) * rows]
    return jnp.dot(window, table, preferred_element_type=F32).astype(BF16)


def left_kernel(meta_ref, tables_ref, own, other, up_1, down_1, up_2, down_2, out_ref, raw):
    cols, rows = own.shape
    z, yl = meta_ref[0], meta_ref[1]
    raw[:, at_block(4 + yl, rows)] = own[...]
    raw[:, at_block(5 - yl, rows)] = other[...]
    for dz, piece in ((-2, up_2), (-1, up_1), (1, down_1), (2, down_2)):
        raw[:, at_block(4 + 2 * dz + yl, rows)] = piece[:cols]
        raw[:, at_block(5 + 2 * dz - yl, rows)] = piece[cols:]
    for i in range(1, 10):
        e = (2 * z + i - 4) & (NE - 1)
        out_ref[:, (i + 1) * rows : (i + 2) * rows] = filter_left(raw, i, e, meta_ref, tables_ref)


def right_kernel(meta_ref, tables_ref, *refs):
    pieces = refs[0:8]
    out_ref, raw = refs[8:]
    rows = tables_ref.shape[1]
    z, x, yh, core = [meta_ref[i] for i in (0, 2, 3, 4)]
    raw[:rows] = jnp.zeros((rows, raw.shape[1]), BF16)
    for q in range(2):
        for s in range(4):
            for dy in range(2):
                line = NYH * ((x + DX[s]) & 3) + (yh ^ dy)
                e = 2 * meta_ref[7 + NZ * z + line] + (core ^ q)
                raw[at_block(e + 1, rows)] = pieces[4 * q + s][dy * rows : (dy + 1) * rows]
    for e in range(NE):
        table = tables_ref[table_of(e, meta_ref)]
        white = jnp.dot(table, raw[e * rows : (e + 2) * rows], preferred_element_type=F32)
        out_ref[at_block((e - 2 * z + 5) & (NE - 1), rows)] = white.astype(BF16)


def most_kernel(meta_ref, tables_ref, left_in, right_ref, up_2, down_2, up_3, down_3, out_ref, left_ref, raw):
    rows = tables_ref.shape[2]
    cols = out_ref.shape[0]
    z, yl = meta_ref[0], meta_ref[1]
    raw[:, :rows] = down_2[at_block(1 ^ yl, cols)]
    raw[:, 5 * rows :] = up_2[at_block(yl, cols)]
    for at, piece in ((1, down_3), (3, up_3)):
        raw[:, at_block(at + yl, rows)] = piece[:cols]
        raw[:, at_block(at + 1 - yl, rows)] = piece[cols:]
    for i, shift in ((1, 5), (2, 5), (4, -9), (5, -9)):
        e = (2 * z + i + shift) & (NE - 1)
        at = (i + shift + 5) % NE * rows
        left_ref[:, at : at + rows] = filter_left(raw, i, e, meta_ref, tables_ref)
    depth = (NE - 3) * rows
    out_ref[...] = jnp.dot(left_ref[:, :depth], right_ref[:depth], preferred_element_type=F32)


def last_kernel(scale, meta_ref, tables_ref, most_ref, right_ref, up_3, down_3, far_own, far_other, out_ref, raw, left):
    cols, rows = far_own.shape
    z, yl = meta_ref[0], meta_ref[1]
    raw[:, :rows] = down_3[at_block(1 ^ yl, cols)]
    raw[:, 3 * rows :] = up_3[at_block(yl, cols)]
    raw[:, at_block(1 + yl, rows)] = far_own[...]
    raw[:, at_block(2 - yl, rows)] = far_other[...]
    for i in range(1, 4):
        e = (2 * z + i + 7) & (NE - 1)
        left[:, (i - 1) * rows : i * rows] = filter_left(raw, i, e, meta_ref, tables_ref)
    right = right_ref[(NE - 3) * rows :]
    out_ref[...] = (most_ref[...] + jnp.dot(left[...], right, preferred_element_type=F32)) * scale


def whitened(kernel, name, meta, tables, pieces, shape, raw_shape):
    vmem = pl.BlockSpec(memory_space=pltpu.VMEM)
    return pl.pallas_call(
        kernel,
        out_shape=jax.ShapeDtypeStruct(shape, BF16),
        in_specs=[pl.BlockSpec(memory_space=pltpu.SMEM)] + [vmem] * (1 + len(pieces)),
        out_specs=vmem,
        scratch_shapes=[pltpu.VMEM(raw_shape, BF16)],
        compiler_params=pltpu.CompilerParams(vmem_limit_bytes=16 * 1024 * 1024),
        name=name,
    )(meta, tables, *pieces)


def most_of_product(meta, tables, left, right, pieces, rows):
    vmem = pl.BlockSpec(memory_space=pltpu.VMEM)
    cols = right.shape[1]
    return pl.pallas_call(
        most_kernel,
        out_shape=[jax.ShapeDtypeStruct((cols, cols), F32), jax.ShapeDtypeStruct(left.shape, BF16)],
        in_specs=[pl.BlockSpec(memory_space=pltpu.SMEM)] + [vmem] * (3 + len(pieces)),
        out_specs=[vmem, vmem],
        scratch_shapes=[pltpu.VMEM((cols, 6 * rows), BF16)],
        input_output_aliases={2: 1},
        compiler_params=pltpu.CompilerParams(vmem_limit_bytes=16 * 1024 * 1024),
        name="most",
    )(meta, tables, left, right, *pieces)[0]


def product(meta, tables, most, right, pieces, rows, scale):
    vmem = pl.BlockSpec(memory_space=pltpu.VMEM)
    cols = right.shape[1]
    return pl.pallas_call(
        functools.partial(last_kernel, scale),
        out_shape=jax.ShapeDtypeStruct((cols, cols), F32),
        in_specs=[pl.BlockSpec(memory_space=pltpu.SMEM)] + [vmem] * (3 + len(pieces)),
        out_specs=vmem,
        scratch_shapes=[pltpu.VMEM((cols, 4 * rows), BF16), pltpu.VMEM((cols, 3 * rows), BF16)],
        compiler_params=pltpu.CompilerParams(vmem_limit_bytes=16 * 1024 * 1024),
        name="product",
    )(meta, tables, most, right, *pieces)


def on_device(partials, gaps, arc_start, taps):
    rows, cols = partials.shape
    places = [lax.axis_index(axis) for axis in EPOCH + COL]
    origin = np.argsort(np.array(LINE, np.int32), axis=0).T.astype(np.int32)
    meta = jnp.stack(places + [arc_start[0], arc_start[0] // rows]).astype(jnp.int32)
    meta = jnp.concatenate([meta, jnp.asarray(origin.reshape(-1))])
    masked, own = prepare(partials, gaps)

    def up(block):
        return around(block, "z", NZ, 1)

    def down(block):
        return around(block, "z", NZ, -1)

    def along_x(block):
        return [around(block, "x", NX, step) for step in (1, -1, 2)]

    def swapped(block):
        return around(block, "c", NC, 1)

    def across(block):
        return around(block, "yh", NYH, 1)

    sync = lax.optimization_barrier
    here = in_plane(masked)
    other = around(own, "yl", NYL, 1)
    up_own, down_own = up(own), down(own)
    here, other, tables = sync((here, other, make_tables(meta, taps, rows)))
    here = along_z(here)
    up_own, down_own, here = sync((up_own, down_own, here))
    up_other, down_other = up(other), down(other)
    up_1 = jnp.concatenate([up_own, up_other], axis=0)
    down_1 = jnp.concatenate([down_own, down_other], axis=0)
    pair = jnp.concatenate([here, across(here)], axis=0)
    up_1, down_1, pair = sync((up_1, down_1, pair))
    up_2, down_2 = up(up_1), down(down_1)
    left = whitened(left_kernel, "left", meta, tables[1], [own, other, up_1, down_1, up_2, down_2], (cols, NE * rows), (cols, 10 * rows))
    mine = [pair] + along_x(pair)
    mine[3], left = sync((mine[3], left))
    up_3, down_3 = up(up_2), down(down_2)
    end_up, end_down = sync((up_3[:cols], down_3[cols:]))
    theirs = [swapped(piece) for piece in mine]
    far_own, far_other = up(end_up), down(end_down)
    right = whitened(right_kernel, "right", meta, tables[0], mine + theirs, (NE * rows, cols), ((NE + 1) * rows, cols))
    most = most_of_product(meta, tables[1], left, right, [up_2, down_2, up_3, down_3], rows)
    return product(meta, tables[1], most, right, [up_3, down_3, far_own, far_other], rows, (rows * NE) ** (-0.5))


def solution(mesh):
    fine = Mesh(mesh.devices.reshape(NZ, NYL, NX, NYH, NC), EPOCH + COL)
    in_specs = (P(EPOCH, COL), P(EPOCH), P(), P())
    return jax.shard_map(on_device, mesh=fine, in_specs=in_specs, out_specs=P(COL, EPOCH), check_vma=False)
```
